256 devices in a mesh: tok: 16 (over z_hi, x, core), exp: 16 (over y, z_lo).
Axes of the slice: x: 4, y: 4, z: 8 (z_hi: 2, z_lo: 4; z = z_hi * 4 + z_lo), core: 2. Of those that a mesh axis runs over, the one named last changes fastest.
Arguments:
- tokens: float32 [12288, 1280], P('tok', 'exp'), may hold values from -6 to 6
- out_grad: float32 [12288, 1280], P('tok', 'exp'), may hold values from -6 to 6
- slot_proj: bfloat16 [1280, 4096], P(None, 'exp'), may hold values from -2 to 2
- weight_in: bfloat16 [16, 1280, 5120], P('exp', None, 'tok'), may hold values from -0.15625 to 0.15625
- weight_out: bfloat16 [16, 5120, 1280], P('exp', 'tok'), may hold values from -0.078125 to 0.078125
- slot_norm: float32 [4096], P('exp'), may hold values from -1 to 6
- token_norm: float32 [12288], P('tok'), may hold values from -1 to 6
Outputs:
- grad_tokens: float32 [12288, 1280], P('tok', 'exp')
- grad_slot_proj: float32 [1280, 4096], P('tok', 'exp')
- grad_weight_in: float32 [16, 1280, 5120], P('exp', None, 'tok')
- grad_weight_out: float32 [16, 5120, 1280], P('exp', 'tok')
The draws below stay inside these ranges and needn't reach their ends.
All inputs are finite; a program needn't handle non-finite values.
Results may differ from the reference program's by a relative error of at most 0.012.
The reference program's roundings to bfloat16 on the way (of `hidden`, `slot_out_half`, `pre_grad` and `slot_in_grad_half`) count: a program that leaves them out, or rounds other values in their place, can miss the bound.
Values may be sent and summed in bfloat16 or wider, within the bound.
A program may use at most 64 MiB of HBM per device.

```python
import jax
import jax.numpy as jnp
from jax import lax

D = 1280
FF = 5120
SLOTS = 256
TOKENS = 12288
EXPERTS = 16


def draw_tokens(key, part):
    values = jnp.clip(jax.random.normal(key, (TOKENS, D), jnp.float32), -6.0, 6.0)
    return values


def draw_slot_proj(key, part):
    spread = 3.0 / jnp.sqrt(jnp.float32(D))
    values = jnp.clip(jax.random.normal(key, (D, EXPERTS * SLOTS), jnp.float32), -4.0, 4.0)
    return (values * spread).astype(jnp.bfloat16)


def draw_slot_norm(key, part):
    values = jax.random.uniform(key, (EXPERTS * SLOTS,), jnp.float32, 4.0, 6.0)
    return values


def draw_token_norm(key, part):
    values = jax.random.uniform(key, (TOKENS,), jnp.float32, 4.0, 6.0)
    return values


def steps_of(rng, dims, split, smallest, high):
    def one(dim, blocks):
        steps = jax.random.uniform(jax.random.fold_in(jax.random.fold_in(rng, 6), dim), (blocks,), jnp.float32, smallest / len(split), high / len(split))
        return jnp.repeat(jnp.exp(steps), dims[dim] // blocks).reshape((-1,) + (1,) * (len(dims) - dim - 1))

    level = one(*split[0])
    for cut in split[1:]:
        level = level * one(*cut)
    return level


def gaussian(rng, shape, width, bound, shards=(), held_as=jnp.bfloat16):
    values = jax.random.normal(rng, shape, jnp.float32) * width
    if len(shards) > 0:
        values = steps_of(rng, shape, shards, -0.22, 0.18) * values
    return jnp.clip(values, min=-bound, max=bound).astype(held_as)


def setup_inputs(seed: int = 0) -> dict:
    streams_of = jax.random.split(jax.random.key(seed), 8)
    tokens = draw_tokens(jax.random.fold_in(streams_of[7], 71), 0)
    out_grad = gaussian(streams_of[1], (TOKENS, D), 1.0, 6.0, ((0, 16), (1, 16)), jnp.float32)
    slot_proj = draw_slot_proj(jax.random.fold_in(streams_of[7], 71), 0)
    weight_in = gaussian(streams_of[3], (EXPERTS, D, FF), D ** -0.5, 0.15625, ((0, 16), (2, 16)))
    weight_out = gaussian(streams_of[4], (EXPERTS, FF, D), FF ** -0.5, 0.078125, ((0, 16), (1, 16)))
    slot_norm = draw_slot_norm(jax.random.fold_in(streams_of[7], 71), 0)
    token_norm = draw_token_norm(jax.random.fold_in(streams_of[7], 71), 0)
    return {"tokens": tokens, "out_grad": out_grad, "slot_proj": slot_proj, "weight_in": weight_in, "weight_out": weight_out, "slot_norm": slot_norm, "token_norm": token_norm}


GELU_C = 0.7978845608028654


def gelu_parts(pre_act):
    inner = GELU_C * (pre_act + 0.044715 * pre_act ** 3)
    tangent = jnp.tanh(inner)
    value = 0.5 * pre_act * (1.0 + tangent)
    slope = 0.5 * (1.0 + tangent) + 0.5 * pre_act * (1.0 - tangent * tangent) * GELU_C * (1.0 + 3.0 * 0.044715 * pre_act * pre_act)
    return value, slope


def weights_of(tok_half, proj_e, norm_e, token_norm):
    logits = jnp.dot(tok_half, proj_e, preferred_element_type=jnp.float32)
    dispatch = jnp.exp(logits - norm_e[None, :]) / jnp.float32(TOKENS)
    combine = jnp.exp(logits - token_norm[:, None]) / jnp.float32(EXPERTS * SLOTS)
    return dispatch, combine


def reference(tokens, out_grad, slot_proj, weight_in, weight_out, slot_norm, token_norm):
    tok_half = tokens.astype(jnp.bfloat16)
    grad_half = out_grad.astype(jnp.bfloat16)
    proj_stack = slot_proj.reshape(D, EXPERTS, SLOTS).transpose(1, 0, 2)
    norm_stack = slot_norm.reshape(EXPERTS, SLOTS)

    def first_pass(items):
        proj_e, norm_e, win_e, wout_e = items
        dispatch, combine = weights_of(tok_half, proj_e, norm_e, token_norm)
        dispatch_half = dispatch.astype(jnp.bfloat16)
        combine_half = combine.astype(jnp.bfloat16)
        slot_in = jnp.dot(dispatch_half.T, tok_half, preferred_element_type=jnp.float32)
        slot_grad = jnp.dot(combine_half.T, grad_half, preferred_element_type=jnp.float32)
        slot_in_half = slot_in.astype(jnp.bfloat16)
        pre_act = jnp.dot(slot_in_half, win_e, preferred_element_type=jnp.float32)
        gelu_out, gelu_slope = gelu_parts(pre_act)
        hidden = gelu_out.astype(jnp.bfloat16)
        slot_out_half = jnp.dot(hidden, wout_e, preferred_element_type=jnp.float32).astype(jnp.bfloat16)
        slot_grad_half = slot_grad.astype(jnp.bfloat16)
        grad_wout = jnp.dot(hidden.T, slot_grad_half, preferred_element_type=jnp.float32)
        hidden_grad = jnp.dot(slot_grad_half, wout_e.T, preferred_element_type=jnp.float32)
        pre_grad = (hidden_grad * gelu_slope).astype(jnp.bfloat16)
        grad_win = jnp.dot(slot_in_half.T, pre_grad, preferred_element_type=jnp.float32)
        slot_in_grad_half = jnp.dot(pre_grad, win_e.T, preferred_element_type=jnp.float32).astype(jnp.bfloat16)
        comb_grad = jnp.dot(grad_half, slot_out_half.T, preferred_element_type=jnp.float32)
        row_part = jnp.sum(combine * comb_grad, axis=1)
        return grad_win, grad_wout, slot_out_half, slot_in_grad_half, row_part

    grad_weight_in, grad_weight_out, outs_half, ingrads_half, row_parts = lax.map(first_pass, (proj_stack, norm_stack, weight_in, weight_out))
    row_stat = jnp.sum(row_parts, axis=0)

    def second_pass(carry, items):
        proj_e, norm_e, out_half, ingrad_half = items
        dispatch, combine = weights_of(tok_half, proj_e, norm_e, token_norm)
        dispatch_half = dispatch.astype(jnp.bfloat16)
        combine_half = combine.astype(jnp.bfloat16)
        comb_grad = jnp.dot(grad_half, out_half.T, preferred_element_type=jnp.float32)
        disp_grad = jnp.dot(tok_half, ingrad_half.T, preferred_element_type=jnp.float32)
        col_stat = jnp.sum(dispatch_half.astype(jnp.float32) * disp_grad, axis=0)
        disp_part = dispatch * (disp_grad - col_stat[None, :])
        inner_grad = (combine * comb_grad + disp_part).astype(jnp.bfloat16)
        logit_grad = (combine * (comb_grad - row_stat[:, None]) + disp_part).astype(jnp.bfloat16)
        proj_grad = jnp.dot(tok_half.T, logit_grad, preferred_element_type=jnp.float32)
        token_term = jnp.dot(inner_grad, proj_e.T, preferred_element_type=jnp.float32)
        token_term = token_term - row_stat[:, None] * jnp.dot(combine_half, proj_e.T, preferred_element_type=jnp.float32)
        token_term = token_term + jnp.dot(dispatch_half, ingrad_half, preferred_element_type=jnp.float32)
        return carry + token_term, proj_grad

    grad_tokens, proj_grads = lax.scan(second_pass, jnp.zeros((TOKENS, D), jnp.float32), (proj_stack, norm_stack, outs_half, ingrads_half))
    grad_slot_proj = proj_grads.transpose(1, 0, 2).reshape(D, EXPERTS * SLOTS)
    return grad_tokens, grad_slot_proj, grad_weight_in, grad_weight_out
```

```python
import functools

import jax
import jax.numpy as jnp
from jax import lax
from jax.experimental import pallas as pl
from jax.experimental.pallas import tpu as pltpu
from jax.sharding import PartitionSpec as P

GELU_C = 0.7978845608028654
MESH = pl.DeviceIdType.MESH
BF = jnp.bfloat16
F32 = jnp.float32
VMEM = pl.BlockSpec(memory_space=pltpu.VMEM)
Y, Z, X, C, H = 4, 4, 4, 2, 2


def rem(a, n):
    return lax.rem(a, n)


class Places:
    def __init__(self):
        e, t = lax.axis_index("exp"), lax.axis_index("tok")
        self.e, self.t = e, t
        self.y, self.z = lax.div(e, Z), rem(e, Z)
        self.h, self.x, self.c = lax.div(t, 8), rem(lax.div(t, 2), X), rem(t, 2)

    def exp_at(self, y, z):
        return {"exp": y * Z + z}

    def y_step(self, k):
        return rem(self.y + k + Y, Y)

    def z_step(self, k):
        return rem(self.z + k + Z, Z)

    def x_step(self, k):
        return rem(self.x + k + X, X)

    def y_peer(self, k):
        return {"exp": self.y_step(k) * Z + self.z}

    def z_peer(self, k):
        return {"exp": self.y * Z + self.z_step(k)}

    def x_peer(self, k):
        return {"tok": self.h * 8 + self.x_step(k) * 2 + self.c}

    def core_peer(self):
        return {"tok": self.h * 8 + self.x * 2 + 1 - self.c}

    def h_peer(self):
        return {"tok": (1 - self.h) * 8 + self.x * 2 + self.c}


class Wire:
    def __init__(self, send_sem, recv_sem):
        self.send_sem, self.recv_sem, self.made = send_sem, recv_sem, []

    def send(self, src, dst, peer):
        k = len(self.made)
        copy = pltpu.make_async_remote_copy(
            src_ref=src,
            dst_ref=dst,
            send_sem=self.send_sem.at[k],
            recv_sem=self.recv_sem.at[k],
            device_id=peer,
            device_id_type=MESH,
        )
        copy.start()
        self.made.append(copy)
        return copy

    def drain(self):
        for copy in self.made:
            copy.wait_send()


def greet(peers):
    barrier = pltpu.get_barrier_semaphore()
    for peer in peers:
        pl.semaphore_signal(barrier, inc=1, device_id=peer, device_id_type=MESH)
    pl.semaphore_wait(barrier, len(peers))


def interleave(*streams):
    live = list(streams)
    while live:
        for s in list(live):
            try:
                next(s)
            except StopIteration:
                live.remove(s)


def call(body, outs, ins, scratch, copies, cid):
    return pl.pallas_call(
        body,
        out_shape=tuple(jax.ShapeDtypeStruct(s, d) for s, d in outs),
        in_specs=[VMEM] * len(ins),
        out_specs=tuple(VMEM for _ in outs),
        scratch_shapes=[
            *scratch,
            pltpu.SemaphoreType.DMA((copies,)),
            pltpu.SemaphoreType.DMA((copies,)),
        ],
        compiler_params=pltpu.CompilerParams(
            collective_id=cid, has_side_effects=True, vmem_limit_bytes=60000 * 1024
        ),
    )(*ins)


def gather_exp_kernel(tok_ref, grad_ref, tok_out, grad_out, send_sem, recv_sem):
    at = Places()
    greet([at.z_peer(k) for k in (1, 2, 3)] + [at.y_peer(k) for k in (1, -1)])
    wire = Wire(send_sem, recv_sem)
    rows = tok_ref.shape[0]
    half = tok_ref.shape[1] // 2

    def block(out, y, z):
        return out.at[pl.ds(pl.multiple_of((y * Z + z) * rows, 16), rows), :]

    def part(out, y, z, side):
        return out.at[
            pl.ds(pl.multiple_of((y * Z + z) * rows, 16), rows), pl.ds(side * half, half)
        ]

    pairs = ((tok_ref, tok_out), (grad_ref, grad_out))
    from_z = [
        [wire.send(src, block(out, at.y, at.z), at.z_peer(k)) for k in (1, 2, 3)]
        for src, out in pairs
    ]
    steps, last = [], []

    def forward(n):
        out, z, right, left = steps[n]
        right.wait_recv()
        spot = part(out, at.y_step(-1), z, 0)
        last.append(wire.send(spot, spot, at.y_peer(1)))
        left.wait_recv()
        spot = part(out, at.y_step(1), z, 1)
        last.append(wire.send(spot, spot, at.y_peer(-1)))

    for a, (src, out) in enumerate(pairs):
        for j in range(4):
            z = at.z_step(-j)
            spot = block(out, at.y, z)
            origin = spot
            if j == 0:
                origin = src
            else:
                from_z[a][j - 1].wait_recv()
            right = wire.send(origin, spot, at.y_peer(1))
            left = wire.send(origin, spot, at.y_peer(-1))
            steps.append((out, z, right, left))
            if len(steps) > 1:
                forward(len(steps) - 2)
        out[pl.ds(pl.multiple_of(at.e * rows, 16), rows), :] = src[...]
    forward(len(steps) - 1)
    for copy in last:
        copy.wait_recv()
    wire.drain()


def gather_exp(tok, grad):
    rows, width = tok.shape
    out = ((rows * 16, width), BF)
    return call(gather_exp_kernel, (out, out), (tok, grad), (), 6 + 32, 0)


def reduced_stream(at, wire, part, out, core_in, sx, xa, x1, sz, zin, keep=None, stat=None):
    rows, width = part.shape
    n = rows // (C * X)
    half = width // 2
    lo, hi = pl.ds(0, half), pl.ds(half, half)
    order = (2, 1, -1, 0)

    def spot(c, k):
        return pl.ds(pl.multiple_of(c * (n * X) + at.x_step(k) * n, 16), n)

    got = []
    for o, k in enumerate(order):
        got.append(wire.send(part.at[spot(1 - at.c, k), :], core_in.at[o], at.core_peer()))
    yield

    def mine(o):
        got[o].wait_recv()
        return part[spot(at.c, order[o]), :] + core_in[o]

    sx[0] = mine(0)
    a = wire.send(sx.at[0, :, lo], xa.at[:, lo], at.x_peer(1))
    b = wire.send(sx.at[0, :, hi], xa.at[:, hi], at.x_peer(-1))
    sx[1] = mine(1)
    early1 = wire.send(sx.at[1, :, hi], x1.at[0, :, hi], at.x_peer(1))
    sx[2] = mine(2)
    early2 = wire.send(sx.at[2, :, lo], x1.at[1, :, lo], at.x_peer(-1))
    yield
    a.wait_recv()
    sx[1, :, :half] = sx[1, :, :half] + xa[:, :half]
    late1 = wire.send(sx.at[1, :, lo], x1.at[0, :, lo], at.x_peer(1))
    b.wait_recv()
    sx[2, :, half:] = sx[2, :, half:] + xa[:, half:]
    late2 = wire.send(sx.at[2, :, hi], x1.at[1, :, hi], at.x_peer(-1))
    sz[...] = mine(3)
    yield
    for copy in (early1, early2, late1, late2):
        copy.wait_recv()
    sz[...] = sz[...] + x1[0] + x1[1]
    swap = wire.send(sz, zin, at.h_peer())
    yield
    swap.wait_recv()
    home = spot(at.c, 0)
    total = sz[...] + zin[...]
    if keep is not None:
        keep[...] = total
    rounded = total.astype(BF)
    out[home, :] = rounded
    boards = [out]
    if stat is not None:
        kept, col = stat
        dots = jnp.sum(rounded.astype(F32) * kept[...], axis=1, keepdims=True)
        col[home, :] = jnp.broadcast_to(dots, (n, col.shape[1]))
        boards.append(col)

    def share(k, peer):
        rows_of = spot(at.c, k)
        return [wire.send(o.at[rows_of, :], o.at[rows_of, :], peer) for o in boards]

    def wait(copies):
        for copy in copies:
            copy.wait_recv()

    right, left = share(0, at.x_peer(1)), share(0, at.x_peer(-1))
    ends = share(0, at.core_peer())
    yield
    wait(right)
    s = spot(at.c, -1)
    fars = [wire.send(out.at[s, lo], out.at[s, lo], at.x_peer(1))]
    if stat is not None:
        fars.append(wire.send(col.at[s, :], col.at[s, :], at.x_peer(1)))
    ends += share(-1, at.core_peer())
    wait(left)
    s = spot(at.c, 1)
    fars.append(wire.send(out.at[s, hi], out.at[s, hi], at.x_peer(-1)))
    ends += share(1, at.core_peer())
    yield
    wait(fars)
    ends += share(2, at.core_peer())
    yield
    wait(ends)


STREAM_COPIES = 4 + 2 + 4 + 1 + 3 + 4 + 1


def stream_scratch(rows, width):
    n = rows // (C * X)
    return (
        pltpu.VMEM((4, n, width), F32),
        pltpu.VMEM((3, n, width), F32),
        pltpu.VMEM((n, width), F32),
        pltpu.VMEM((2, n, width), F32),
        pltpu.VMEM((n, width), F32),
        pltpu.VMEM((n, width), F32),
    )


def tok_peers(at):
    return [at.core_peer(), at.x_peer(1), at.x_peer(-1), at.h_peer()]


def reduce_in_kernel(p0, p1, o0, o1, keep, *rest):
    s0, s1, (send_sem, recv_sem) = rest[:6], rest[6:12], rest[12:]
    at = Places()
    greet(tok_peers(at))
    wire = Wire(send_sem, recv_sem)
    interleave(
        reduced_stream(at, wire, p0, o0, *s0, keep=keep),
        reduced_stream(at, wire, p1, o1, *s1),
    )
    wire.drain()


def reduce_out_kernel(p0, p1, kept, o0, o1, col, *rest):
    s0, s1, (send_sem, recv_sem) = rest[:6], rest[6:12], rest[12:]
    at = Places()
    greet(tok_peers(at))
    wire = Wire(send_sem, recv_sem)
    interleave(
        reduced_stream(at, wire, p0, o0, *s0),
        reduced_stream(at, wire, p1, o1, *s1, stat=(kept, col)),
    )
    wire.drain()


def reduce_in(p0, p1):
    out = (p0.shape, BF)
    kept = ((p0.shape[0] // (C * X), p0.shape[1]), F32)
    scratch = stream_scratch(*p0.shape) + stream_scratch(*p1.shape)
    return call(reduce_in_kernel, (out, out, kept), (p0, p1), scratch, 2 * STREAM_COPIES, 1)


def reduce_out(p0, p1, kept):
    out = (p0.shape, BF)
    col = ((p0.shape[0], 128), F32)
    scratch = stream_scratch(*p0.shape) + stream_scratch(*p1.shape)
    return call(
        reduce_out_kernel, (out, out, col), (p0, p1, kept), scratch, 2 * STREAM_COPIES + 7, 2
    )


def sum_exp_kernel(v_ref, out, buf, send_sem, recv_sem):
    at = Places()
    peers = [{"exp": rem(at.e + k, Y * Z)} for k in range(1, Y * Z)]
    greet(peers)
    wire = Wire(send_sem, recv_sem)
    copies = [wire.send(v_ref, buf.at[at.e], peer) for peer in peers]
    buf[at.e] = v_ref[...]
    for copy in copies:
        copy.wait_recv()
    out[...] = jnp.sum(buf[...], axis=0)
    wire.drain()


def sum_exp(v):
    return call(
        sum_exp_kernel, ((v.shape, F32),), (v,), (pltpu.VMEM((16, *v.shape), F32),), 15, 3
    )[0]


def scatter_exp_stream(at, wire, part, out, sbuf, ya, y1, y2, sz, zin):
    rows, width = out.shape
    half = width // 2
    lo, hi = pl.ds(0, half), pl.ds(half, half)
    order = (1, 2, 3, 0)

    def spot(dy, j):
        e = at.y_step(dy) * Z + at.z_step(order[j])
        return pl.ds(pl.multiple_of(e * rows, 16), rows)

    first, early, late = [], [], []
    for j in range(4):
        sbuf[j, 0] = part[spot(2, j), :].astype(BF)
        first.append(
            (
                wire.send(sbuf.at[j, 0, :, lo], ya.at[j, :, lo], at.y_peer(1)),
                wire.send(sbuf.at[j, 0, :, hi], ya.at[j, :, hi], at.y_peer(-1)),
            )
        )
        sbuf[j, 1, :, half:] = part[spot(1, j), hi].astype(BF)
        sbuf[j, 2, :, :half] = part[spot(-1, j), lo].astype(BF)
        early.append(
            (
                wire.send(sbuf.at[j, 1, :, hi], y1.at[j, :, hi], at.y_peer(1)),
                wire.send(sbuf.at[j, 2, :, lo], y2.at[j, :, lo], at.y_peer(-1)),
            )
        )
    yield
    tail = []

    def finish(j):
        for copy in early[j] + late[j]:
            copy.wait_recv()
        total = part[spot(0, j), :] + y1[j].astype(F32) + y2[j].astype(F32)
        if order[j] == 0:
            out[...] = total
        else:
            sz[j] = total.astype(BF)
            tail.append(wire.send(sz.at[j], zin.at[j], at.z_peer(order[j])))

    for j in range(4):
        first[j][0].wait_recv()
        sbuf[j, 1, :, :half] = (part[spot(1, j), lo] + ya[j, :, :half].astype(F32)).astype(BF)
        right = wire.send(sbuf.at[j, 1, :, lo], y1.at[j, :, lo], at.y_peer(1))
        first[j][1].wait_recv()
        sbuf[j, 2, :, half:] = (part[spot(-1, j), hi] + ya[j, :, half:].astype(F32)).astype(BF)
        left = wire.send(sbuf.at[j, 2, :, hi], y2.at[j, :, hi], at.y_peer(-1))
        late.append((right, left))
        yield
        if j >= 1:
            finish(j - 1)
            yield
    finish(3)
    yield
    for copy in tail:
        copy.wait_recv()
    out[...] = out[...] + zin[0].astype(F32) + zin[1].astype(F32) + zin[2].astype(F32)


def scatter_tok_stream(at, wire, part, out, send1, core_in, sx, xa, x1, sz, zin):
    order = (2, 1, -1, 0)
    got = []
    for o, k in enumerate(order):
        for h in range(H):
            send1[o, h] = part[h, at.x_step(k), 1 - at.c].astype(BF)
        got.append(wire.send(send1.at[o], core_in.at[o], at.core_peer()))
    yield
    for copy in got:
        copy.wait_recv()

    def mine(o, h):
        return part[h, at.x_step(order[o]), at.c] + core_in[o, h].astype(F32)

    for h in range(H):
        sx[0, h] = mine(0, h).astype(BF)
    a = wire.send(sx.at[0, 0], xa.at[0], at.x_peer(1))
    b = wire.send(sx.at[0, 1], xa.at[1], at.x_peer(-1))
    sx[1, 1] = mine(1, 1).astype(BF)
    sx[2, 0] = mine(2, 0).astype(BF)
    early1 = wire.send(sx.at[1, 1], x1.at[0, 1], at.x_peer(1))
    early2 = wire.send(sx.at[2, 0], x1.at[1, 0], at.x_peer(-1))
    yield
    a.wait_recv()
    sx[1, 0] = (mine(1, 0) + xa[0].astype(F32)).astype(BF)
    late1 = wire.send(sx.at[1, 0], x1.at[0, 0], at.x_peer(1))
    b.wait_recv()
    sx[2, 1] = (mine(2, 1) + xa[1].astype(F32)).astype(BF)
    late2 = wire.send(sx.at[2, 1], x1.at[1, 1], at.x_peer(-1))
    yield
    for copy in (early1, early2, late1, late2):
        copy.wait_recv()

    def total(h):
        own = part[h, at.x, at.c] + core_in[3, h].astype(F32)
        return own + x1[0, h].astype(F32) + x1[1, h].astype(F32)

    sz[...] = total(1 - at.h).astype(BF)
    swap = wire.send(sz, zin, at.h_peer())
    out[...] = total(at.h)
    yield
    yield
    yield
    swap.wait_recv()
    out[...] = out[...] + zin[...].astype(F32)


def scatter_kernel(tok_part, proj_part, tok_out, proj_out, *rest):
    s0, s1, (send_sem, recv_sem) = rest[:6], rest[6:13], rest[13:]
    at = Places()
    greet(
        [at.z_peer(k) for k in (1, 2, 3)] + [at.y_peer(k) for k in (1, -1)] + tok_peers(at)
    )
    wire = Wire(send_sem, recv_sem)
    interleave(
        scatter_exp_stream(at, wire, tok_part, tok_out, *s0),
        scatter_tok_stream(at, wire, proj_part, proj_out, *s1),
    )
    wire.drain()


def scatter(tok_part, proj_part):
    rows, width = tok_part.shape[0] // 16, tok_part.shape[1]
    prows, pwidth = proj_part.shape[0] // 16, proj_part.shape[1]
    v = lambda *s: pltpu.VMEM(s, BF)
    scratch = (
        v(4, 3, rows, width),
        v(4, rows, width),
        v(4, rows, width),
        v(4, rows, width),
        v(3, rows, width),
        v(3, rows, width),
        v(4, H, prows, pwidth),
        v(4, H, prows, pwidth),
        v(3, H, prows, pwidth),
        v(H, prows, pwidth),
        v(2, H, prows, pwidth),
        v(prows, pwidth),
        v(prows, pwidth),
    )
    outs = (((rows, width), F32), ((prows, pwidth), F32))
    blocks = proj_part.reshape(H, X, C, prows, pwidth)
    return call(scatter_kernel, outs, (tok_part, blocks), scratch, 16 + 8 + 3 + 4 + 6 + 1, 4)


def gelu_parts(pre_act):
    inner = GELU_C * (pre_act + 0.044715 * pre_act**3)
    tangent = jnp.tanh(inner)
    value = 0.5 * pre_act * (1.0 + tangent)
    slope = 0.5 * (1.0 + tangent) + 0.5 * pre_act * (1.0 - tangent * tangent) * GELU_C * (
        1.0 + 3.0 * 0.044715 * pre_act * pre_act
    )
    return (value, slope)


dot = functools.partial(jnp.einsum, preferred_element_type=jnp.float32)


def local(tokens, out_grad, slot_proj, weight_in, weight_out, slot_norm, token_norm):
    w_in, w_out = weight_in[0], weight_out[0]
    tok, grad = gather_exp(tokens.astype(BF).T, out_grad.astype(BF).T)
    tok_total = tok.shape[1] * lax.axis_size("tok")
    all_slots = slot_proj.shape[1] * lax.axis_size("exp")
    logits = dot("ds,dn->sn", slot_proj, tok)
    dispatch = jnp.exp(logits - slot_norm[:, None]) / jnp.float32(tok_total)
    combine = jnp.exp(logits - token_norm[None, :]) / jnp.float32(all_slots)
    dispatch_half, combine_half = dispatch.astype(BF), combine.astype(BF)
    slot_in_half, slot_grad_half, kept = reduce_in(
        dot("sn,dn->sd", dispatch_half, tok), dot("sn,dn->sd", combine_half, grad)
    )
    pre_act = dot("sd,df->sf", slot_in_half, w_in)
    gelu_out, gelu_slope = gelu_parts(pre_act)
    hidden = gelu_out.astype(BF)
    hidden_grad = dot("sd,fd->sf", slot_grad_half, w_out)
    pre_grad = (hidden_grad * gelu_slope).astype(BF)
    slot_out_half, slot_in_grad_half, col = reduce_out(
        dot("sf,fd->sd", hidden, w_out), dot("sf,df->sd", pre_grad, w_in), kept
    )
    grad_weight_out = dot("sf,sd->fd", hidden, slot_grad_half)
    grad_weight_in = dot("sd,sf->df", slot_in_half, pre_grad)
    comb_grad = dot("sd,dn->sn", slot_out_half, grad)
    row_part = jnp.sum(combine * comb_grad, axis=0)
    row_stat = sum_exp(row_part[None, :])
    disp_grad = dot("sd,dn->sn", slot_in_grad_half, tok)
    disp_part = dispatch * (disp_grad - col[:, :1])
    inner_grad = (combine * comb_grad + disp_part).astype(BF)
    logit_grad = (combine * (comb_grad - row_stat) + disp_part).astype(BF)
    token_term = (
        dot("ds,sn->dn", slot_proj, inner_grad)
        - row_stat * dot("ds,sn->dn", slot_proj, combine_half)
        + dot("sd,sn->dn", slot_in_grad_half, dispatch_half)
    )
    proj_part = dot("dn,sn->ds", tok, logit_grad)
    grad_tokens, grad_slot_proj = scatter(token_term, proj_part)
    return (grad_tokens.T, grad_slot_proj, grad_weight_in[None], grad_weight_out[None])


def solution(mesh):
    return jax.shard_map(
        local,
        mesh=mesh,
        in_specs=(
            P("tok", "exp"),
            P("tok", "exp"),
            P(None, "exp"),
            P("exp", None, "tok"),
            P("exp", "tok", None),
            P("exp"),
            P("tok"),
        ),
        out_specs=(P("tok", "exp"), P("tok", "exp"), P("exp", None, "tok"), P("exp", "tok", None)),
        check_vma=False,
    )
```

```python
import functools

import jax
import jax.numpy as jnp
from jax import lax
from jax.experimental import pallas as pl
from jax.experimental.pallas import tpu as pltpu
from jax.sharding import PartitionSpec as P

GELU_C = 0.7978845608028654
MESH = pl.DeviceIdType.MESH
BF = jnp.bfloat16
F32 = jnp.float32
VMEM = pl.BlockSpec(memory_space=pltpu.VMEM)
Y, Z, X, C, H = 4, 4, 4, 2, 2


def rem(a, n):
    return lax.rem(a, n)


class Places:
    def __init__(self):
        e, t = lax.axis_index("exp"), lax.axis_index("tok")
        self.e, self.t = e, t
        self.y, self.z = lax.div(e, Z), rem(e, Z)
        self.h, self.x, self.c = lax.div(t, 8), rem(lax.div(t, 2), X), rem(t, 2)

    def exp_at(self, y, z):
        return {"exp": y * Z + z}

    def y_step(self, k):
        return rem(self.y + k + Y, Y)

    def z_step(self, k):
        return rem(self.z + k + Z, Z)

    def x_step(self, k):
        return rem(self.x + k + X, X)

    def y_peer(self, k):
        return {"exp": self.y_step(k) * Z + self.z}

    def z_peer(self, k):
        return {"exp": self.y * Z + self.z_step(k)}

    def x_peer(self, k):
        return {"tok": self.h * 8 + self.x_step(k) * 2 + self.c}

    def core_peer(self):
        return {"tok": self.h * 8 + self.x * 2 + 1 - self.c}

    def z_swap(self, j):
        if j == 1:
            return self.z + 1 - 2 * rem(self.z, 2)
        return (self.z, None, rem(self.z + 2, Z), Z - 1 - self.z)[j]

    def z_pair(self, j):
        return {"exp": self.y * Z + self.z_swap(j)}

    def everyone(self):
        peers = [self.z_pair(k) for k in (1, 2, 3)] + [self.y_peer(k) for k in (1, -1, 2)]
        return peers + [self.core_peer(), self.x_peer(1), self.x_peer(-1), self.x_peer(2), self.h_peer()]

    def h_peer(self):
        return {"tok": (1 - self.h) * 8 + self.x * 2 + self.c}


class Wire:
    def __init__(self, send_sem, recv_sem):
        self.send_sem, self.recv_sem, self.made = send_sem, recv_sem, []

    def send(self, src, dst, peer):
        k = len(self.made)
        copy = pltpu.make_async_remote_copy(
            src_ref=src,
            dst_ref=dst,
            send_sem=self.send_sem.at[k],
            recv_sem=self.recv_sem.at[k],
            device_id=peer,
            device_id_type=MESH,
        )
        copy.start()
        self.made.append(copy)
        return copy

    def drain(self):
        for copy in self.made:
            copy.wait_send()


def greet(peers):
    barrier = pltpu.get_barrier_semaphore()
    for peer in peers:
        pl.semaphore_signal(barrier, inc=1, device_id=peer, device_id_type=MESH)
    pl.semaphore_wait(barrier, len(peers))


def wait_all(copies):
    for copy in copies:
        copy.wait_recv()


def gather(at, wire, src, out, from_z):
    rows, width = src.shape
    half = width // 2

    def spot(y, z, *lanes):
        return out.at[(pl.ds(pl.multiple_of((y * Z + z) * rows, 16), rows), *lanes)]

    steps, last = [], []

    def forward():
        z, right, left = steps[len(last) // 2]
        right.wait_recv()
        s = spot(at.y_step(-1), z, pl.ds(0, half))
        last.append(wire.send(s, s, at.y_peer(1)))
        left.wait_recv()
        s = spot(at.y_step(1), z, pl.ds(half, half))
        last.append(wire.send(s, s, at.y_peer(-1)))

    def start(j):
        z = at.z_swap(j)
        s = spot(at.y, z)
        if j > 0:
            from_z[j - 1].wait_recv()
        origin = src if j == 0 else s
        steps.append((z, wire.send(origin, s, at.y_peer(1)), wire.send(origin, s, at.y_peer(-1))))

    start(0)
    yield
    out[pl.ds(pl.multiple_of(at.e * rows, 16), rows), :] = src[...]
    forward()
    yield
    start(1)
    yield
    start(2)
    yield
    forward()
    yield
    start(3)
    yield
    forward()
    yield
    forward()
    yield
    wait_all(last)


def z_sends(at, wire, src, out, sent):
    rows = src.shape[0]
    s = out.at[pl.ds(pl.multiple_of(at.e * rows, 16), rows), :]
    sent += [wire.send(src, s, at.z_pair(k)) for k in (1, 2, 3)]
    yield


def ring_sum(at, wire, r, mine, half, sx, xa, x1, sz):
    lo, hi = pl.ds(0, half), pl.ds(half, sx.shape[-1] - half)
    sx[r, 0] = mine(0)
    a = wire.send(sx.at[r, 0, :, lo], xa.at[r, :, lo], at.x_peer(1))
    b = wire.send(sx.at[r, 0, :, hi], xa.at[r, :, hi], at.x_peer(-1))
    sx[r, 1] = mine(1)
    early1 = wire.send(sx.at[r, 1, :, hi], x1.at[r, 0, :, hi], at.x_peer(1))
    sx[r, 2] = mine(2)
    early2 = wire.send(sx.at[r, 2, :, lo], x1.at[r, 1, :, lo], at.x_peer(-1))
    yield
    a.wait_recv()
    sx[r, 1, :, :half] = sx[r, 1, :, :half] + xa[r, :, :half]
    late1 = wire.send(sx.at[r, 1, :, lo], x1.at[r, 0, :, lo], at.x_peer(1))
    b.wait_recv()
    sx[r, 2, :, half:] = sx[r, 2, :, half:] + xa[r, :, half:]
    late2 = wire.send(sx.at[r, 2, :, hi], x1.at[r, 1, :, hi], at.x_peer(-1))
    sz[r] = mine(3)
    yield
    wait_all((early1, early2, late1, late2))
    sz[r] = sz[r] + x1[r, 0] + x1[r, 1]


def reduced(at, wire, r, part, out, core_in, sx, xa, x1, sz, zin, keep=None, stat=None):
    rows, width = part.shape
    full = rows // (C * X)
    n = full // 2
    half = -(-width // 256) * 128
    order = (2, 1, -1, 0)

    def spot(c, k):
        return pl.ds(pl.multiple_of(c * (full * X) + at.x_step(k) * full + r * n, 16), n)

    got = [
        wire.send(part.at[spot(1 - at.c, k), :], core_in.at[r, o], at.core_peer())
        for o, k in enumerate(order)
    ]
    yield

    def mine(o):
        got[o].wait_recv()
        return part[spot(at.c, order[o]), :] + core_in[r, o]

    yield from ring_sum(at, wire, r, mine, half, sx, xa, x1, sz)
    swap = wire.send(sz.at[r], zin.at[r], at.h_peer())
    yield
    swap.wait_recv()
    home = spot(at.c, 0)
    total = sz[r] + zin[r]
    if keep is not None:
        keep[r] = total
    rounded = total.astype(BF)
    out[home, :] = rounded
    boards = [out]
    if stat is not None:
        kept, col = stat
        dots = jnp.sum(rounded.astype(F32) * kept[r], axis=1, keepdims=True)
        col[home, :] = jnp.broadcast_to(dots, (n, col.shape[1]))
        boards.append(col)

    def share(k, peer):
        rows_of = spot(at.c, k)
        return [wire.send(o.at[rows_of, :], o.at[rows_of, :], peer) for o in boards]

    spread = [(k, share(0, at.x_peer(k))) for k in (1, -1, 2)]
    ends = share(0, at.core_peer())
    yield
    for k, copies in spread:
        wait_all(copies)
        ends += share(-k, at.core_peer())
        if k != 1:
            yield
    wait_all(ends)


Q = 2
STREAM_COPIES = 4 + 2 + 4 + 1 + 3 + 4


def stream_scratch(rows, width):
    n = rows // (C * X * 2)
    f = lambda *s: pltpu.VMEM((*s, n, width), F32)
    return (f(2, 4), f(2, 3), f(2), f(2, 2), f(2), f(2))


def sum_exp(at, wire, value, partial, out, zbuf, ybuf):
    copies = [wire.send(value, zbuf.at[k - 1], at.z_pair(k)) for k in (1, 2, 3)]
    yield
    wait_all(copies)
    partial[...] = value[...] + zbuf[0] + zbuf[1] + zbuf[2]
    copies = [wire.send(partial, ybuf.at[i], at.y_peer(k)) for i, k in enumerate((1, -1, 2))]
    yield
    wait_all(copies)
    out[...] = partial[...] + ybuf[0] + ybuf[1] + ybuf[2]


def scatter_exp(at, wire, fill, part, out, sbuf, ya, y1, y2, sz, zin):
    rows, width = out.shape
    half = width // 2
    lo, hi = pl.ds(0, half), pl.ds(half, half)
    order = (3, 2, 1, 0)

    def spot(dy, j):
        e = at.y_step(dy) * Z + at.z_swap(order[j])
        return pl.ds(pl.multiple_of(e * rows, 16), rows)

    first, early, late = [[], [], [], []], [], []
    for lanes, side, peer in ((lo, 0, at.y_peer(1)), (hi, half, at.y_peer(-1))):
        fill(2, lanes)
        for j in range(4):
            sbuf[j, 0, :, side : side + half] = part[spot(2, j), lanes].astype(BF)
            first[j].append(wire.send(sbuf.at[j, 0, :, lanes], ya.at[j, :, lanes], peer))
        yield
    for lanes in (lo, hi):
        fill(1, lanes)
        fill(-1, lanes)
    for j in range(4):
        sbuf[j, 1, :, half:] = part[spot(1, j), hi].astype(BF)
        sbuf[j, 2, :, :half] = part[spot(-1, j), lo].astype(BF)
        early.append(
            (
                wire.send(sbuf.at[j, 1, :, hi], y1.at[j, :, hi], at.y_peer(1)),
                wire.send(sbuf.at[j, 2, :, lo], y2.at[j, :, lo], at.y_peer(-1)),
            )
        )
        first[j][0].wait_recv()
        sbuf[j, 1, :, :half] = (part[spot(1, j), lo] + ya[j, :, :half].astype(F32)).astype(BF)
        right = wire.send(sbuf.at[j, 1, :, lo], y1.at[j, :, lo], at.y_peer(1))
        first[j][1].wait_recv()
        sbuf[j, 2, :, half:] = (part[spot(-1, j), hi] + ya[j, :, half:].astype(F32)).astype(BF)
        left = wire.send(sbuf.at[j, 2, :, hi], y2.at[j, :, hi], at.y_peer(-1))
        late.append((right, left))
        yield
    for lanes in (lo, hi):
        fill(0, lanes)
    tail = []
    for j in range(4):
        yield
        wait_all(early[j] + late[j])
        total = part[spot(0, j), :] + y1[j].astype(F32) + y2[j].astype(F32)
        if order[j] == 0:
            out[...] = total
        else:
            sz[j] = total.astype(BF)
            tail.append(wire.send(sz.at[j], zin.at[j], at.z_pair(order[j])))
    yield
    wait_all(tail)
    out[...] = out[...] + zin[0].astype(F32) + zin[1].astype(F32) + zin[2].astype(F32)


def scatter_tok(at, wire, part, out, core_in, sx, xa, x1, sz, zin):
    rows = out.shape[0]
    order = (2, 1, -1, 0)

    def spot(h, k, c):
        t = h * 8 + at.x_step(k) * 2 + c
        return pl.ds(pl.multiple_of(t * rows, 16), rows)

    got = [
        [
            wire.send(part.at[spot(h, k, 1 - at.c), :], core_in.at[o, h], at.core_peer())
            for h in range(H)
        ]
        for o, k in enumerate(order)
    ]
    yield
    for copies in got:
        wait_all(copies)

    def mine(o, h):
        return part[spot(h, order[o], at.c), :] + core_in[o, h]

    for h in range(H):
        sx[0, h] = mine(0, h).astype(BF)
    a = wire.send(sx.at[0, 0], xa.at[0], at.x_peer(1))
    b = wire.send(sx.at[0, 1], xa.at[1], at.x_peer(-1))
    sx[1, 1] = mine(1, 1).astype(BF)
    sx[2, 0] = mine(2, 0).astype(BF)
    early1 = wire.send(sx.at[1, 1], x1.at[0, 1], at.x_peer(1))
    early2 = wire.send(sx.at[2, 0], x1.at[1, 0], at.x_peer(-1))
    yield
    a.wait_recv()
    sx[1, 0] = (mine(1, 0) + xa[0].astype(F32)).astype(BF)
    late1 = wire.send(sx.at[1, 0], x1.at[0, 0], at.x_peer(1))
    b.wait_recv()
    sx[2, 1] = (mine(2, 1) + xa[1].astype(F32)).astype(BF)
    late2 = wire.send(sx.at[2, 1], x1.at[1, 1], at.x_peer(-1))
    yield
    wait_all((early1, early2, late1, late2))

    def total(h):
        own = part[spot(h, 0, at.c), :] + core_in[3, h]
        return own + x1[0, h].astype(F32) + x1[1, h].astype(F32)

    sz[...] = total(1 - at.h).astype(BF)
    swap = wire.send(sz, zin, at.h_peer())
    out[...] = total(at.h)
    yield
    swap.wait_recv()
    out[...] = out[...] + zin[...].astype(F32)


def gelu_parts(pre_act):
    inner = GELU_C * (pre_act + 0.044715 * pre_act**3)
    tangent = jnp.tanh(inner)
    value = 0.5 * pre_act * (1.0 + tangent)
    slope = 0.5 * (1.0 + tangent) + 0.5 * pre_act * (1.0 - tangent * tangent) * GELU_C * (
        1.0 + 3.0 * 0.044715 * pre_act * pre_act
    )
    return (value, slope)


def nn(a, b):
    return lax.dot_general(a, b, (((1,), (0,)), ((), ())), preferred_element_type=F32)


def nt(a, b):
    return lax.dot_general(a, b, (((1,), (1,)), ((), ())), preferred_element_type=F32)


def tiles(count, size, body):
    def go(i, carry):
        body(pl.ds(pl.multiple_of(i * size, size), size))
        return carry

    lax.fori_loop(0, count, go, 0)


def advance(*gens):
    for g in gens:
        next(g, None)


ORDER = (
    "TZ", "T", "tg", "G", "GZ", "turn", "T", "T", "G", "T", "T", "T", "T", "T", "G", "G",
    "T", "c1", "G", "G", "c2", "S1", "G", "S1", "G", "S1", "G", "c3", "S2", "m2", "S1", "S2",
    "S2", "S1", "S1", "S2", "S1", "S1", "c4", "c5", "C1", "S2", "C1", "S2", "C1", "S2", "S2", "c6",
    "c7", "C2", "C1", "C2", "C2", "C1", "C1", "C2", "C1", "C1", "c8", "R", "C2", "R", "C2", "R",
    "C2", "C2", "c8t", "c9a", "E", "c9b", "E", "c11", "F", "E", "E", "F", "E", "E", "F", "E",
    "E", "F", "E", "E", "F", "E", "E",
)


def kernel(
    x_in,
    g_in,
    proj_hbm,
    w_in_hbm,
    w_out_hbm,
    slot_norm,
    token_norm,
    grad_tokens,
    grad_proj,
    slot_in,
    slot_grad,
    hidden,
    pre_grad,
    *rest,
):
    rest = list(rest)

    def take(n=1):
        got = rest[:n]
        del rest[:n]
        return got if n > 1 else got[0]

    x_ref, g_ref, tok, grad, both, proj_t, w_in, w_out = take(8)
    dispatch, combine, mixed, comb_half = take(4)
    parts = take(4)
    slope, slot_out, slot_in_grad, kept, col = take(5)
    cross, weighted, base, logit_half, term, proj_part = take(6)
    streams = [take(6) for _ in range(4 * Q)]
    row, row_sum, row_stat, token_row, zbuf, ybuf = take(6)
    e_bufs = take(6)
    f_bufs = take(6)
    local_sem, send_sem, recv_sem = take(3)
    slots = slot_norm.shape[0]
    tokens = token_norm.shape[0]
    width = tok.shape[0]
    tok_total = jnp.float32(tokens * X * C * H)
    all_slots = jnp.float32(slots * Y * Z)
    proj = both.at[:, pl.ds(0, slots)]
    disp_half = mixed.at[pl.ds(slots, slots), :]
    inner_half = mixed.at[pl.ds(0, slots), :]

    loads = [
        pltpu.make_async_copy(proj_hbm, proj, local_sem.at[0]),
        pltpu.make_async_copy(w_in_hbm, w_in, local_sem.at[1]),
        pltpu.make_async_copy(w_out_hbm, w_out, local_sem.at[2]),
    ]
    for load in loads:
        load.start()
    at = Places()
    x_ref[...] = x_in[...].astype(BF)
    greet(at.everyone())
    wire = Wire(send_sem, recv_sem)

    def halves(i, out, **more):
        gens = []
        for q in range(Q):
            cols = pl.ds(q * (width // Q), width // Q)
            args = (parts[i].at[:, cols], out.at[:, cols], *streams[i * Q + q])
            opts = {}
            if "keep" in more:
                opts["keep"] = kept.at[q]
            if "stat" in more:
                opts["stat"] = (kept.at[q], col.at[q])
            gens += [reduced(at, wire, r, *args, **opts) for r in range(2)]
        return gens

    def fill(k, cols):
        rows = pl.ds(pl.multiple_of(at.y_step(k) * (width // Y), 16), width // Y)
        new = nn(both[rows, :], mixed[:, cols])
        term[rows, cols] = new - row_stat[:, cols] * cross[rows, cols]

    tok_z, grad_z = [], []
    gens = {
        "TZ": [z_sends(at, wire, x_ref, tok, tok_z)],
        "GZ": [z_sends(at, wire, g_ref, grad, grad_z)],
        "T": [gather(at, wire, x_ref, tok, tok_z)],
        "G": [gather(at, wire, g_ref, grad, grad_z)],
        "S1": halves(0, slot_in, keep=True),
        "S2": halves(1, slot_grad),
        "C1": halves(2, slot_out),
        "C2": halves(3, slot_in_grad, stat=True),
        "R": [sum_exp(at, wire, row, row_sum, row_stat, zbuf, ybuf)],
        "E": [scatter_exp(at, wire, fill, term, grad_tokens, *e_bufs)],
        "F": [scatter_tok(at, wire, proj_part, grad_proj, *f_bufs)],
    }

    def c1():
        token_row[...] = token_norm[...].reshape(1, tokens)
        slot_shift = jnp.broadcast_to(slot_norm[...].reshape(1, slots), (128, slots)).T[:, :1]

        def go(cols):
            logits = nn(proj_t[...], tok[:, cols])
            d = jnp.exp(logits - slot_shift) / tok_total
            c = jnp.exp(logits - token_row[:, cols]) / all_slots
            dispatch[:, cols] = d
            combine[:, cols] = c
            mixed[pl.ds(slots, slots), cols] = d.astype(BF)
            comb_half[:, cols] = c.astype(BF)

        tiles(3, 256, go)

    def c2():
        def go(rows):
            parts[0][:, rows] = nt(disp_half[...], tok[rows, :])

        tiles(5, 256, go)

    def c3():
        def go(rows):
            parts[1][:, rows] = nt(comb_half[...], grad[rows, :])

        tiles(5, 256, go)

    def m2():
        def go(rows):
            cross[rows, :] = nn(both[rows, pl.ds(0, slots)], comb_half[...])

        tiles(5, 256, go)

    def c4():
        loads[1].wait()
        value, s = gelu_parts(nt(slot_in[...], w_in[...]))
        hidden[...] = value.astype(BF)
        slope[...] = s

    def c5():
        loads[2].wait()

        def go(cols):
            parts[2][:, cols] = nn(hidden[...], w_out[:, cols])

        tiles(5, 256, go)

    def c6():
        pre_grad[...] = (nt(slot_grad[...], w_out[...]) * slope[...]).astype(BF)

    def c7():
        def go(cols):
            parts[3][:, cols] = nn(pre_grad[...], w_in[:, cols])

        tiles(5, 256, go)

    def c8():
        def go(cols):
            w = combine[:, cols] * nn(slot_out[...], grad[:, cols])
            weighted[:, cols] = w
            row[:, cols] = jnp.sum(w, axis=0, keepdims=True)

        tiles(3, 256, go)

    def c8t():
        def go(cols):
            both[cols, pl.ds(slots, slots)] = slot_in_grad[:, cols].T

        tiles(5, 256, go)

    def c9(i):
        cols = pl.ds(i * (tokens // 2), tokens // 2)
        disp_grad = nn(slot_in_grad[...], tok[:, cols])
        b = weighted[:, cols] + dispatch[:, cols] * (disp_grad - col[0, :, :1] - col[1, :, :1])
        base[:, cols] = b
        mixed[pl.ds(0, slots), cols] = b.astype(BF)

    def c11():
        def make(cols):
            logit_half[:, cols] = (base[:, cols] - combine[:, cols] * row_stat[:, cols]).astype(BF)

        tiles(3, 256, make)

        def go(rows):
            proj_part[rows, :] = nt(tok[rows, :], logit_half[...])

        tiles(5, 256, go)

    def turn():
        loads[0].wait()

        def go(rows):
            proj_t[:, rows] = both[rows, pl.ds(0, slots)].T

        tiles(5, 256, go)

    def tg():
        g_ref[...] = g_in[...].astype(BF)

    work = dict(turn=turn, tg=tg, c1=c1, c2=c2, c3=c3, c4=c4, c5=c5, c6=c6, c7=c7, c8=c8, c8t=c8t, c9a=lambda: c9(0), c9b=lambda: c9(1), c11=c11, m2=m2)
    for name in ORDER:
        if name in work:
            work[name]()
        else:
            advance(*gens[name])
    assert all(next(g, None) is None and g.gi_frame is None for gs in gens.values() for g in gs)
    wire.drain()


def fused(x, g, slot_proj, w_in, w_out, slot_norm, token_norm):
    rows, n = x.shape
    width, slots = slot_proj.shape
    ff = w_in.shape[0]
    prows = width // 16
    b = lambda *s: pltpu.VMEM(s, BF)
    f = lambda *s: pltpu.VMEM(s, F32)
    part = f(slots, width)
    scratch = (
        *(b(rows, n), b(rows, n)),
        *(b(width, n), b(width, n), b(width, 2 * slots), b(slots, width), b(ff, width), b(ff, width)),
        *(f(slots, n), f(slots, n), b(2 * slots, n), b(slots, n)),
        *(part, part, part, part),
        *(f(slots, ff), b(slots, width), b(slots, width), f(Q, 2, slots // 16, width // Q), f(Q, slots, 128)),
        *(f(width, n), f(slots, n), f(slots, n), b(slots, n), f(width, n), f(width, slots)),
        *(stream_scratch(slots, width // Q) * (4 * Q)),
        *(f(1, n), f(1, n), f(1, n), f(1, n), f(3, 1, n), f(3, 1, n)),
        *(b(4, 3, rows, n), b(4, rows, n), b(4, rows, n), b(4, rows, n), b(3, rows, n), b(3, rows, n)),
        f(4, H, prows, slots),
        *(b(3, H, prows, slots), b(H, prows, slots), b(2, H, prows, slots)),
        *(b(prows, slots), b(prows, slots)),
    )
    copies = 38 + 8 * Q * STREAM_COPIES + 14 * Q + 6 + 27 + 15
    any_space = pl.BlockSpec(memory_space=pl.ANY)
    outs = (
        ((rows, n), F32),
        ((prows, slots), F32),
        ((slots, width), BF),
        ((slots, width), BF),
        ((slots, ff), BF),
        ((slots, ff), BF),
    )
    return pl.pallas_call(
        kernel,
        out_shape=tuple(jax.ShapeDtypeStruct(s, d) for s, d in outs),
        in_specs=[VMEM, VMEM, any_space, any_space, any_space, VMEM, VMEM],
        out_specs=tuple(VMEM for _ in outs),
        scratch_shapes=[
            *scratch,
            pltpu.SemaphoreType.DMA((3,)),
            pltpu.SemaphoreType.DMA((copies,)),
            pltpu.SemaphoreType.DMA((copies,)),
        ],
        compiler_params=pltpu.CompilerParams(
            collective_id=0, has_side_effects=True, vmem_limit_bytes=60000 * 1024
        ),
    )(x, g, slot_proj, w_in, w_out, slot_norm, token_norm)


dot = functools.partial(jnp.einsum, preferred_element_type=jnp.float32)


def local(tokens, out_grad, slot_proj, weight_in, weight_out, slot_norm, token_norm):
    grad_tokens, grad_slot_proj, slot_in, slot_grad, hidden, pre_grad = fused(
        tokens.T,
        out_grad.T,
        slot_proj,
        weight_in[0].T,
        weight_out[0],
        slot_norm,
        token_norm,
    )
    grad_weight_out = dot("sf,sd->fd", hidden, slot_grad)
    grad_weight_in = dot("sd,sf->df", slot_in, pre_grad)
    return (grad_tokens.T, grad_slot_proj, grad_weight_in[None], grad_weight_out[None])


def solution(mesh):
    return jax.shard_map(
        local,
        mesh=mesh,
        in_specs=(
            P("tok", "exp"),
            P("tok", "exp"),
            P(None, "exp"),
            P("exp", None, "tok"),
            P("exp", "tok", None),
            P("exp"),
            P("tok"),
        ),
        out_specs=(P("tok", "exp"), P("tok", "exp"), P("exp", None, "tok"), P("exp", "tok", None)),
        check_vma=False,
    )
```

```python
import functools

import jax
import jax.numpy as jnp
from jax import lax
from jax.experimental import pallas as pl
from jax.experimental.pallas import tpu as pltpu
from jax.sharding import PartitionSpec as P

GELU_C = 0.7978845608028654
MESH = pl.DeviceIdType.MESH
BF = jnp.bfloat16
F32 = jnp.float32
VMEM = pl.BlockSpec(memory_space=pltpu.VMEM)
Y, Z, X, C, H = 4, 4, 4, 2, 2


def rem(a, n):
    return lax.rem(a, n)


class Places:
    def __init__(self):
        e, t = lax.axis_index("exp"), lax.axis_index("tok")
        self.e, self.t = e, t
        self.y, self.z = lax.div(e, Z), rem(e, Z)
        self.h, self.x, self.c = lax.div(t, 8), rem(lax.div(t, 2), X), rem(t, 2)

    def exp_at(self, y, z):
        return {"exp": y * Z + z}

    def y_step(self, k):
        return rem(self.y + k + Y, Y)

    def z_step(self, k):
        return rem(self.z + k + Z, Z)

    def x_step(self, k):
        return rem(self.x + k + X, X)

    def y_peer(self, k):
        return {"exp": self.y_step(k) * Z + self.z}

    def z_peer(self, k):
        return {"exp": self.y * Z + self.z_step(k)}

    def x_peer(self, k):
        return {"tok": self.h * 8 + self.x_step(k) * 2 + self.c}

    def core_peer(self):
        return {"tok": self.h * 8 + self.x * 2 + 1 - self.c}

    def z_swap(self, j):
        if j == 1:
            return self.z + 1 - 2 * rem(self.z, 2)
        return (self.z, None, rem(self.z + 2, Z), Z - 1 - self.z)[j]

    def z_pair(self, j):
        return {"exp": self.y * Z + self.z_swap(j)}

    def everyone(self):
        peers = [self.z_pair(k) for k in (1, 2, 3)] + [self.y_peer(k) for k in (1, -1, 2)]
        return peers + [self.core_peer(), self.x_peer(1), self.x_peer(-1), self.x_peer(2), self.h_peer()]

    def h_peer(self):
        return {"tok": (1 - self.h) * 8 + self.x * 2 + self.c}


class Wire:
    def __init__(self, send_sem, recv_sem):
        self.send_sem, self.recv_sem, self.made = send_sem, recv_sem, []

    def send(self, src, dst, peer):
        k = len(self.made)
        copy = pltpu.make_async_remote_copy(
            src_ref=src,
            dst_ref=dst,
            send_sem=self.send_sem.at[k],
            recv_sem=self.recv_sem.at[k],
            device_id=peer,
            device_id_type=MESH,
        )
        copy.start()
        self.made.append(copy)
        return copy

    def drain(self):
        for copy in self.made:
            copy.wait_send()


def greet(peers):
    barrier = pltpu.get_barrier_semaphore()
    for peer in peers:
        pl.semaphore_signal(barrier, inc=1, device_id=peer, device_id_type=MESH)
    pl.semaphore_wait(barrier, len(peers))


def wait_all(copies):
    for copy in copies:
        copy.wait_recv()


def gather(at, wire, src, out, from_z):
    rows, width = src.shape
    half = width // 2

    def spot(y, z, *lanes):
        return out.at[(pl.ds(pl.multiple_of((y * Z + z) * rows, 16), rows), *lanes)]

    steps, last = [], []

    def forward():
        z, right, left = steps[len(last) // 2]
        right.wait_recv()
        s = spot(at.y_step(-1), z, pl.ds(0, half))
        last.append(wire.send(s, s, at.y_peer(1)))
        left.wait_recv()
        s = spot(at.y_step(1), z, pl.ds(half, half))
        last.append(wire.send(s, s, at.y_peer(-1)))

    def start(j):
        z = at.z_swap(j)
        s = spot(at.y, z)
        if j > 0:
            from_z[j - 1].wait_recv()
        origin = src if j == 0 else s
        steps.append((z, wire.send(origin, s, at.y_peer(1)), wire.send(origin, s, at.y_peer(-1))))

    start(0)
    yield
    out[pl.ds(pl.multiple_of(at.e * rows, 16), rows), :] = src[...]
    forward()
    yield
    start(1)
    yield
    start(2)
    yield
    forward()
    yield
    start(3)
    yield
    forward()
    yield
    forward()
    yield
    wait_all(last)


def z_sends(at, wire, src, out, sent):
    rows = src.shape[0]
    s = out.at[pl.ds(pl.multiple_of(at.e * rows, 16), rows), :]
    sent += [wire.send(src, s, at.z_pair(k)) for k in (1, 2, 3)]
    yield


def ring_sum(at, wire, r, mine, half, sx, xa, x1, sz):
    lo, hi = pl.ds(0, half), pl.ds(half, sx.shape[-1] - half)
    sx[r, 0] = mine(0)
    a = wire.send(sx.at[r, 0, :, lo], xa.at[r, :, lo], at.x_peer(1))
    b = wire.send(sx.at[r, 0, :, hi], xa.at[r, :, hi], at.x_peer(-1))
    sx[r, 1] = mine(1)
    early1 = wire.send(sx.at[r, 1, :, hi], x1.at[r, 0, :, hi], at.x_peer(1))
    sx[r, 2] = mine(2)
    early2 = wire.send(sx.at[r, 2, :, lo], x1.at[r, 1, :, lo], at.x_peer(-1))
    yield
    a.wait_recv()
    sx[r, 1, :, :half] = sx[r, 1, :, :half] + xa[r, :, :half]
    late1 = wire.send(sx.at[r, 1, :, lo], x1.at[r, 0, :, lo], at.x_peer(1))
    b.wait_recv()
    sx[r, 2, :, half:] = sx[r, 2, :, half:] + xa[r, :, half:]
    late2 = wire.send(sx.at[r, 2, :, hi], x1.at[r, 1, :, hi], at.x_peer(-1))
    sz[r] = mine(3)
    yield
    wait_all((early1, early2, late1, late2))
    sz[r] = sz[r] + x1[r, 0] + x1[r, 1]


def reduced(at, wire, r, part, out, core_in, sx, xa, x1, sz, zin, keep=None, stat=None):
    rows, width = part.shape
    full = rows // (C * X)
    n = full // 2
    half = -(-width // 256) * 128
    order = (2, 1, -1, 0)

    def spot(c, k):
        return pl.ds(pl.multiple_of(c * (full * X) + at.x_step(k) * full + r * n, 16), n)

    got = [
        wire.send(part.at[spot(1 - at.c, k), :], core_in.at[r, o], at.core_peer())
        for o, k in enumerate(order)
    ]
    yield

    def mine(o):
        got[o].wait_recv()
        return part[spot(at.c, order[o]), :] + core_in[r, o]

    yield from ring_sum(at, wire, r, mine, half, sx, xa, x1, sz)
    swap = wire.send(sz.at[r], zin.at[r], at.h_peer())
    yield
    swap.wait_recv()
    home = spot(at.c, 0)
    total = sz[r] + zin[r]
    if keep is not None:
        keep[r] = total
    rounded = total.astype(BF)
    out[home, :] = rounded
    boards = [out]
    if stat is not None:
        kept, col = stat
        dots = jnp.sum(rounded.astype(F32) * kept[r], axis=1, keepdims=True)
        col[home, :] = jnp.broadcast_to(dots, (n, col.shape[1]))
        boards.append(col)

    def share(k, peer):
        rows_of = spot(at.c, k)
        return [wire.send(o.at[rows_of, :], o.at[rows_of, :], peer) for o in boards]

    spread = [(k, share(0, at.x_peer(k))) for k in (1, -1, 2)]
    ends = share(0, at.core_peer())
    yield
    for k, copies in spread:
        wait_all(copies)
        ends += share(-k, at.core_peer())
        if k != 1:
            yield
    wait_all(ends)


Q = 1
STREAM_COPIES = 4 + 2 + 4 + 1 + 3 + 4


def stream_scratch(rows, width):
    n = rows // (C * X * 2)
    f = lambda *s: pltpu.VMEM((*s, n, width), F32)
    return (f(2, 4), f(2, 3), f(2), f(2, 2), f(2), f(2))


def sum_exp(at, wire, value, partial, out, zbuf, ybuf):
    copies = [wire.send(value, zbuf.at[k - 1], at.z_pair(k)) for k in (1, 2, 3)]
    yield
    wait_all(copies)
    partial[...] = value[...] + zbuf[0] + zbuf[1] + zbuf[2]
    copies = [wire.send(partial, ybuf.at[i], at.y_peer(k)) for i, k in enumerate((1, -1, 2))]
    yield
    wait_all(copies)
    out[...] = partial[...] + ybuf[0] + ybuf[1] + ybuf[2]


def scatter_exp(at, wire, fill, part, out, sbuf, ya, y1, y2, sz, zin):
    rows, width = out.shape
    half = width // 2
    lo, hi = pl.ds(0, half), pl.ds(half, half)
    order = (3, 2, 1, 0)

    def spot(dy, j):
        e = at.y_step(dy) * Z + at.z_swap(order[j])
        return pl.ds(pl.multiple_of(e * rows, 16), rows)

    first, early, late = [[], [], [], []], [], []
    for lanes, side, peer in ((lo, 0, at.y_peer(1)), (hi, half, at.y_peer(-1))):
        fill(2, lanes)
        for j in range(4):
            sbuf[j, 0, :, side : side + half] = part[spot(2, j), lanes].astype(BF)
            first[j].append(wire.send(sbuf.at[j, 0, :, lanes], ya.at[j, :, lanes], peer))
        yield
    for lanes in (lo, hi):
        fill(1, lanes)
        fill(-1, lanes)
    for j in range(4):
        sbuf[j, 1, :, half:] = part[spot(1, j), hi].astype(BF)
        sbuf[j, 2, :, :half] = part[spot(-1, j), lo].astype(BF)
        early.append(
            (
                wire.send(sbuf.at[j, 1, :, hi], y1.at[j, :, hi], at.y_peer(1)),
                wire.send(sbuf.at[j, 2, :, lo], y2.at[j, :, lo], at.y_peer(-1)),
            )
        )
        first[j][0].wait_recv()
        sbuf[j, 1, :, :half] = (part[spot(1, j), lo] + ya[j, :, :half].astype(F32)).astype(BF)
        right = wire.send(sbuf.at[j, 1, :, lo], y1.at[j, :, lo], at.y_peer(1))
        first[j][1].wait_recv()
        sbuf[j, 2, :, half:] = (part[spot(-1, j), hi] + ya[j, :, half:].astype(F32)).astype(BF)
        left = wire.send(sbuf.at[j, 2, :, hi], y2.at[j, :, hi], at.y_peer(-1))
        late.append((right, left))
        yield
    for lanes in (lo, hi):
        fill(0, lanes)
    tail = []
    for j in range(4):
        yield
        wait_all(early[j] + late[j])
        total = part[spot(0, j), :] + y1[j].astype(F32) + y2[j].astype(F32)
        if order[j] == 0:
            out[...] = total
        else:
            sz[j] = total.astype(BF)
            tail.append(wire.send(sz.at[j], zin.at[j], at.z_pair(order[j])))
    yield
    wait_all(tail)
    out[...] = out[...] + zin[0].astype(F32) + zin[1].astype(F32) + zin[2].astype(F32)


def scatter_tok(at, wire, part, out, core_in, sx, xa, x1, sz, zin):
    rows = out.shape[0]
    order = (2, 1, -1, 0)

    def spot(h, k, c):
        t = h * 8 + at.x_step(k) * 2 + c
        return pl.ds(pl.multiple_of(t * rows, 16), rows)

    got = [
        [
            wire.send(part.at[spot(h, k, 1 - at.c), :], core_in.at[o, h], at.core_peer())
            for h in range(H)
        ]
        for o, k in enumerate(order)
    ]
    yield
    for copies in got:
        wait_all(copies)

    def mine(o, h):
        return part[spot(h, order[o], at.c), :] + core_in[o, h]

    for h in range(H):
        sx[0, h] = mine(0, h).astype(BF)
    a = wire.send(sx.at[0, 0], xa.at[0], at.x_peer(1))
    b = wire.send(sx.at[0, 1], xa.at[1], at.x_peer(-1))
    sx[1, 1] = mine(1, 1).astype(BF)
    sx[2, 0] = mine(2, 0).astype(BF)
    early1 = wire.send(sx.at[1, 1], x1.at[0, 1], at.x_peer(1))
    early2 = wire.send(sx.at[2, 0], x1.at[1, 0], at.x_peer(-1))
    yield
    a.wait_recv()
    sx[1, 0] = (mine(1, 0) + xa[0].astype(F32)).astype(BF)
    late1 = wire.send(sx.at[1, 0], x1.at[0, 0], at.x_peer(1))
    b.wait_recv()
    sx[2, 1] = (mine(2, 1) + xa[1].astype(F32)).astype(BF)
    late2 = wire.send(sx.at[2, 1], x1.at[1, 1], at.x_peer(-1))
    yield
    wait_all((early1, early2, late1, late2))

    def total(h):
        own = part[spot(h, 0, at.c), :] + core_in[3, h]
        return own + x1[0, h].astype(F32) + x1[1, h].astype(F32)

    sz[...] = total(1 - at.h).astype(BF)
    swap = wire.send(sz, zin, at.h_peer())
    out[...] = total(at.h)
    yield
    swap.wait_recv()
    out[...] = out[...] + zin[...].astype(F32)


def gelu_parts(pre_act):
    inner = GELU_C * (pre_act + 0.044715 * pre_act**3)
    tangent = jnp.tanh(inner)
    value = 0.5 * pre_act * (1.0 + tangent)
    slope = 0.5 * (1.0 + tangent) + 0.5 * pre_act * (1.0 - tangent * tangent) * GELU_C * (
        1.0 + 3.0 * 0.044715 * pre_act * pre_act
    )
    return (value, slope)


def nn(a, b):
    return lax.dot_general(a, b, (((1,), (0,)), ((), ())), preferred_element_type=F32)


def nt(a, b):
    return lax.dot_general(a, b, (((1,), (1,)), ((), ())), preferred_element_type=F32)


def tiles(count, size, body):
    def go(i, carry):
        body(pl.ds(pl.multiple_of(i * size, size), size))
        return carry

    lax.fori_loop(0, count, go, 0)


def advance(*gens):
    for g in gens:
        next(g, None)


ORDER = (
    "TZ", "T", "tg", "G", "GZ", "turn", "T", "T", "G", "T", "T", "T", "T", "T", "G", "G",
    "T", "c1", "G", "G", "c2", "S1", "G", "S1", "G", "S1", "G", "c3", "S2", "m2", "S1", "S2",
    "S2", "S1", "S1", "S2", "S1", "S1", "c4", "c5", "C1", "S2", "C1", "S2", "C1", "S2", "S2", "c6",
    "c7", "C2", "put", "C1", "C2", "C2", "C1", "C1", "C2", "C1", "C1", "c8", "R", "C2", "R", "C2",
    "R", "C2", "C2", "c8t", "c9a", "E", "c9b", "E", "c11", "F", "E", "E", "F", "E", "E", "F",
    "E", "E", "F", "E", "E", "F", "E", "E",
)


def kernel(
    x_in,
    g_in,
    proj_hbm,
    w_in_hbm,
    w_out_hbm,
    slot_norm,
    token_norm,
    grad_tokens,
    grad_proj,
    slot_in_out,
    slot_grad_out,
    hidden_out,
    pre_grad_out,
    *rest,
):
    rest = list(rest)

    def take(n=1):
        got = rest[:n]
        del rest[:n]
        return got if n > 1 else got[0]

    x_ref, g_ref, tok, grad, both, proj_t, w_in, w_out = take(8)
    dispatch, combine, mixed, comb_half = take(4)
    parts = take(4)
    slot_in, slot_grad, hidden, pre_grad = take(4)
    slope, slot_out, slot_in_grad, kept, col = take(5)
    cross, weighted, base, logit_half, term, proj_part = take(6)
    streams = [take(6) for _ in range(4 * Q)]
    row, row_sum, row_stat, token_row, zbuf, ybuf = take(6)
    e_bufs = take(6)
    f_bufs = take(6)
    local_sem, send_sem, recv_sem = take(3)
    slots = slot_norm.shape[0]
    tokens = token_norm.shape[0]
    width = tok.shape[0]
    tok_total = jnp.float32(tokens * X * C * H)
    all_slots = jnp.float32(slots * Y * Z)
    proj = both.at[:, pl.ds(0, slots)]
    disp_half = mixed.at[pl.ds(slots, slots), :]
    inner_half = mixed.at[pl.ds(0, slots), :]

    loads = [
        pltpu.make_async_copy(proj_hbm, proj, local_sem.at[0]),
        pltpu.make_async_copy(w_in_hbm, w_in, local_sem.at[1]),
        pltpu.make_async_copy(w_out_hbm, w_out, local_sem.at[2]),
    ]
    for load in loads:
        load.start()
    at = Places()
    x_ref[...] = x_in[...].astype(BF)
    greet(at.everyone())
    wire = Wire(send_sem, recv_sem)

    def halves(i, out, **more):
        gens = []
        for q in range(Q):
            cols = pl.ds(q * (width // Q), width // Q)
            args = (parts[i].at[:, cols], out.at[:, cols], *streams[i * Q + q])
            opts = {}
            if "keep" in more:
                opts["keep"] = kept.at[q]
            if "stat" in more:
                opts["stat"] = (kept.at[q], col.at[q])
            gens += [reduced(at, wire, r, *args, **opts) for r in range(2)]
        return gens

    def fill(k, cols):
        rows = pl.ds(pl.multiple_of(at.y_step(k) * (width // Y), 16), width // Y)
        new = nn(both[rows, :], mixed[:, cols])
        term[rows, cols] = new - row_stat[:, cols] * cross[rows, cols]

    tok_z, grad_z = [], []
    gens = {
        "TZ": [z_sends(at, wire, x_ref, tok, tok_z)],
        "GZ": [z_sends(at, wire, g_ref, grad, grad_z)],
        "T": [gather(at, wire, x_ref, tok, tok_z)],
        "G": [gather(at, wire, g_ref, grad, grad_z)],
        "S1": halves(0, slot_in, keep=True),
        "S2": halves(1, slot_grad),
        "C1": halves(2, slot_out),
        "C2": halves(3, slot_in_grad, stat=True),
        "R": [sum_exp(at, wire, row, row_sum, row_stat, zbuf, ybuf)],
        "E": [scatter_exp(at, wire, fill, term, grad_tokens, *e_bufs)],
        "F": [scatter_tok(at, wire, proj_part, grad_proj, *f_bufs)],
    }

    def c1():
        token_row[...] = token_norm[...].reshape(1, tokens)
        slot_shift = jnp.broadcast_to(slot_norm[...].reshape(1, slots), (128, slots)).T[:, :1]

        def go(cols):
            logits = nn(proj_t[...], tok[:, cols])
            d = jnp.exp(logits - slot_shift) / tok_total
            c = jnp.exp(logits - token_row[:, cols]) / all_slots
            dispatch[:, cols] = d
            combine[:, cols] = c
            mixed[pl.ds(slots, slots), cols] = d.astype(BF)
            comb_half[:, cols] = c.astype(BF)

        tiles(3, 256, go)

    def c2():
        def go(rows):
            parts[0][:, rows] = nt(disp_half[...], tok[rows, :])

        tiles(5, 256, go)

    def c3():
        def go(rows):
            parts[1][:, rows] = nt(comb_half[...], grad[rows, :])

        tiles(5, 256, go)

    def m2():
        def go(rows):
            cross[rows, :] = nn(both[rows, pl.ds(0, slots)], comb_half[...])

        tiles(5, 256, go)

    def c4():
        loads[1].wait()
        value, s = gelu_parts(nt(slot_in[...], w_in[...]))
        hidden[...] = value.astype(BF)
        slope[...] = s

    def c5():
        loads[2].wait()

        def go(cols):
            parts[2][:, cols] = nn(hidden[...], w_out[:, cols])

        tiles(5, 256, go)

    def c6():
        pre_grad[...] = (nt(slot_grad[...], w_out[...]) * slope[...]).astype(BF)

    def c7():
        def go(cols):
            parts[3][:, cols] = nn(pre_grad[...], w_in[:, cols])

        tiles(5, 256, go)

    def c8():
        def go(cols):
            w = combine[:, cols] * nn(slot_out[...], grad[:, cols])
            weighted[:, cols] = w
            row[:, cols] = jnp.sum(w, axis=0, keepdims=True)

        tiles(3, 256, go)

    def c8t():
        def go(cols):
            both[cols, pl.ds(slots, slots)] = slot_in_grad[:, cols].T

        tiles(5, 256, go)

    def c9(i):
        cols = pl.ds(i * (tokens // 2), tokens // 2)
        disp_grad = nn(slot_in_grad[...], tok[:, cols])
        b = weighted[:, cols] + dispatch[:, cols] * (disp_grad - jnp.sum(col[...], axis=0)[:, :1])
        base[:, cols] = b
        mixed[pl.ds(0, slots), cols] = b.astype(BF)

    def c11():
        def make(cols):
            logit_half[:, cols] = (base[:, cols] - combine[:, cols] * row_stat[:, cols]).astype(BF)

        tiles(3, 256, make)

        def go(rows):
            proj_part[rows, :] = nt(tok[rows, :], logit_half[...])

        tiles(5, 256, go)

    def turn():
        loads[0].wait()

        def go(rows):
            proj_t[:, rows] = both[rows, pl.ds(0, slots)].T

        tiles(5, 256, go)

    def tg():
        g_ref[...] = g_in[...].astype(BF)

    kept_for_weights = (
        (slot_in, slot_in_out),
        (slot_grad, slot_grad_out),
        (hidden, hidden_out),
        (pre_grad, pre_grad_out),
    )
    stores = [
        pltpu.make_async_copy(held, out, local_sem.at[3 + i])
        for i, (held, out) in enumerate(kept_for_weights)
    ]

    def put():
        for store in stores:
            store.start()

    work = dict(put=put, turn=turn, tg=tg, c1=c1, c2=c2, c3=c3, c4=c4, c5=c5, c6=c6, c7=c7, c8=c8, c8t=c8t, c9a=lambda: c9(0), c9b=lambda: c9(1), c11=c11, m2=m2)
    for name in ORDER:
        if name in work:
            work[name]()
        else:
            advance(*gens[name])
    assert all(next(g, None) is None and g.gi_frame is None for gs in gens.values() for g in gs)
    for store in stores:
        store.wait()
    wire.drain()


def fused(x, g, slot_proj, w_in, w_out, slot_norm, token_norm):
    rows, n = x.shape
    width, slots = slot_proj.shape
    ff = w_in.shape[0]
    prows = width // 16
    b = lambda *s: pltpu.VMEM(s, BF)
    f = lambda *s: pltpu.VMEM(s, F32)
    part = f(slots, width)
    scratch = (
        *(b(rows, n), b(rows, n)),
        *(b(width, n), b(width, n), b(width, 2 * slots), b(slots, width), b(ff, width), b(ff, width)),
        *(f(slots, n), f(slots, n), b(2 * slots, n), b(slots, n)),
        *(part, part, part, part),
        *(b(slots, width), b(slots, width), b(slots, ff), b(slots, ff)),
        *(f(slots, ff), b(slots, width), b(slots, width), f(Q, 2, slots // 16, width // Q), f(Q, slots, 128)),
        *(f(width, n), f(slots, n), f(slots, n), b(slots, n), f(width, n), f(width, slots)),
        *(stream_scratch(slots, width // Q) * (4 * Q)),
        *(f(1, n), f(1, n), f(1, n), f(1, n), f(3, 1, n), f(3, 1, n)),
        *(b(4, 3, rows, n), b(4, rows, n), b(4, rows, n), b(4, rows, n), b(3, rows, n), b(3, rows, n)),
        f(4, H, prows, slots),
        *(b(3, H, prows, slots), b(H, prows, slots), b(2, H, prows, slots)),
        *(b(prows, slots), b(prows, slots)),
    )
    copies = 38 + 8 * Q * STREAM_COPIES + 14 * Q + 6 + 27 + 15
    any_space = pl.BlockSpec(memory_space=pl.ANY)
    outs = (
        ((rows, n), F32),
        ((prows, slots), F32),
        ((slots, width), BF),
        ((slots, width), BF),
        ((slots, ff), BF),
        ((slots, ff), BF),
    )
    return pl.pallas_call(
        kernel,
        out_shape=tuple(jax.ShapeDtypeStruct(s, d) for s, d in outs),
        in_specs=[VMEM, VMEM, any_space, any_space, any_space, VMEM, VMEM],
        out_specs=(VMEM, VMEM, any_space, any_space, any_space, any_space),
        scratch_shapes=[
            *scratch,
            pltpu.SemaphoreType.DMA((7,)),
            pltpu.SemaphoreType.DMA((copies,)),
            pltpu.SemaphoreType.DMA((copies,)),
        ],
        compiler_params=pltpu.CompilerParams(
            collective_id=0, has_side_effects=True, vmem_limit_bytes=60000 * 1024
        ),
    )(x, g, slot_proj, w_in, w_out, slot_norm, token_norm)


dot = functools.partial(jnp.einsum, preferred_element_type=jnp.float32)


def local(tokens, out_grad, slot_proj, weight_in, weight_out, slot_norm, token_norm):
    grad_tokens, grad_slot_proj, slot_in, slot_grad, hidden, pre_grad = fused(
        tokens.T,
        out_grad.T,
        slot_proj,
        weight_in[0].T,
        weight_out[0],
        slot_norm,
        token_norm,
    )
    grad_weight_out = dot("sf,sd->fd", hidden, slot_grad)
    grad_weight_in = dot("sd,sf->df", slot_in, pre_grad)
    return (grad_tokens.T, grad_slot_proj, grad_weight_in[None], grad_weight_out[None])


def solution(mesh):
    return jax.shard_map(
        local,
        mesh=mesh,
        in_specs=(
            P("tok", "exp"),
            P("tok", "exp"),
            P(None, "exp"),
            P("exp", None, "tok"),
            P("exp", "tok", None),
            P("exp"),
            P("tok"),
        ),
        out_specs=(P("tok", "exp"), P("tok", "exp"), P("exp", None, "tok"), P("exp", "tok", None)),
        check_vma=False,
    )
```

```python
import functools

import jax
import jax.numpy as jnp
from jax import lax
from jax.experimental import pallas as pl
from jax.experimental.pallas import tpu as pltpu
from jax.sharding import PartitionSpec as P

GELU_C = 0.7978845608028654
MESH = pl.DeviceIdType.MESH
BF = jnp.bfloat16
F32 = jnp.float32
VMEM = pl.BlockSpec(memory_space=pltpu.VMEM)
Y, Z, X, C, H = 4, 4, 4, 2, 2


def rem(a, n):
    return lax.rem(a, n)


class Places:
    def __init__(self):
        e, t = lax.axis_index("exp"), lax.axis_index("tok")
        self.e, self.t = e, t
        self.y, self.z = lax.div(e, Z), rem(e, Z)
        self.h, self.x, self.c = lax.div(t, 8), rem(lax.div(t, 2), X), rem(t, 2)

    def exp_at(self, y, z):
        return {"exp": y * Z + z}

    def y_step(self, k):
        return rem(self.y + k + Y, Y)

    def z_step(self, k):
        return rem(self.z + k + Z, Z)

    def x_step(self, k):
        return rem(self.x + k + X, X)

    def y_peer(self, k):
        return {"exp": self.y_step(k) * Z + self.z}

    def z_peer(self, k):
        return {"exp": self.y * Z + self.z_step(k)}

    def x_peer(self, k):
        return {"tok": self.h * 8 + self.x_step(k) * 2 + self.c}

    def core_peer(self):
        return {"tok": self.h * 8 + self.x * 2 + 1 - self.c}

    def z_swap(self, j):
        if j == 1:
            return self.z + 1 - 2 * rem(self.z, 2)
        return (self.z, None, rem(self.z + 2, Z), Z - 1 - self.z)[j]

    def z_pair(self, j):
        return {"exp": self.y * Z + self.z_swap(j)}

    def everyone(self):
        peers = [self.z_pair(k) for k in (1, 2, 3)] + [self.y_peer(k) for k in (1, -1, 2)]
        return peers + [self.core_peer(), self.x_peer(1), self.x_peer(-1), self.x_peer(2), self.h_peer()]

    def h_peer(self):
        return {"tok": (1 - self.h) * 8 + self.x * 2 + self.c}


class Wire:
    def __init__(self, send_sem, recv_sem):
        self.send_sem, self.recv_sem, self.made = send_sem, recv_sem, []

    def send(self, src, dst, peer):
        k = len(self.made)
        copy = pltpu.make_async_remote_copy(
            src_ref=src,
            dst_ref=dst,
            send_sem=self.send_sem.at[k],
            recv_sem=self.recv_sem.at[k],
            device_id=peer,
            device_id_type=MESH,
        )
        copy.start()
        self.made.append(copy)
        return copy

    def drain(self):
        for copy in self.made:
            copy.wait_send()


def greet(peers):
    barrier = pltpu.get_barrier_semaphore()
    for peer in peers:
        pl.semaphore_signal(barrier, inc=1, device_id=peer, device_id_type=MESH)
    pl.semaphore_wait(barrier, len(peers))


def wait_all(copies):
    for copy in copies:
        copy.wait_recv()


def gather(at, wire, src, out, from_z):
    rows, width = src.shape
    half = width // 2

    def spot(y, z, *lanes):
        return out.at[(pl.ds(pl.multiple_of((y * Z + z) * rows, 16), rows), *lanes)]

    steps, last = [], []

    def forward():
        z, right, left = steps[len(last) // 2]
        right.wait_recv()
        s = spot(at.y_step(-1), z, pl.ds(0, half))
        last.append(wire.send(s, s, at.y_peer(1)))
        left.wait_recv()
        s = spot(at.y_step(1), z, pl.ds(half, half))
        last.append(wire.send(s, s, at.y_peer(-1)))

    def start(j):
        z = at.z_swap(j)
        s = spot(at.y, z)
        if j > 0:
            from_z[j - 1].wait_recv()
        origin = src if j == 0 else s
        steps.append((z, wire.send(origin, s, at.y_peer(1)), wire.send(origin, s, at.y_peer(-1))))

    start(0)
    yield
    out[pl.ds(pl.multiple_of(at.e * rows, 16), rows), :] = src[...]
    forward()
    yield
    start(1)
    yield
    start(2)
    yield
    forward()
    yield
    start(3)
    yield
    forward()
    yield
    forward()
    yield
    wait_all(last)


def z_sends(at, wire, src, out, sent):
    rows = src.shape[0]
    s = out.at[pl.ds(pl.multiple_of(at.e * rows, 16), rows), :]
    sent += [wire.send(src, s, at.z_pair(k)) for k in (1, 2, 3)]
    yield


def ring_sum(at, wire, r, mine, half, sx, xa, x1, sz):
    lo, hi = pl.ds(0, half), pl.ds(half, sx.shape[-1] - half)
    sx[r, 0] = mine(0)
    a = wire.send(sx.at[r, 0, :, lo], xa.at[r, :, lo], at.x_peer(1))
    b = wire.send(sx.at[r, 0, :, hi], xa.at[r, :, hi], at.x_peer(-1))
    sx[r, 1] = mine(1)
    early1 = wire.send(sx.at[r, 1, :, hi], x1.at[r, 0, :, hi], at.x_peer(1))
    sx[r, 2] = mine(2)
    early2 = wire.send(sx.at[r, 2, :, lo], x1.at[r, 1, :, lo], at.x_peer(-1))
    yield
    a.wait_recv()
    sx[r, 1, :, :half] = sx[r, 1, :, :half] + xa[r, :, :half]
    late1 = wire.send(sx.at[r, 1, :, lo], x1.at[r, 0, :, lo], at.x_peer(1))
    b.wait_recv()
    sx[r, 2, :, half:] = sx[r, 2, :, half:] + xa[r, :, half:]
    late2 = wire.send(sx.at[r, 2, :, hi], x1.at[r, 1, :, hi], at.x_peer(-1))
    sz[r] = mine(3)
    yield
    wait_all((early1, early2, late1, late2))
    sz[r] = sz[r] + x1[r, 0] + x1[r, 1]


def reduced(at, wire, r, part, out, core_in, sx, xa, x1, sz, zin, keep=None, stat=None):
    rows, width = part.shape
    full = rows // (C * X)
    n = full // 2
    half = -(-width // 256) * 128
    order = (2, 1, -1, 0)

    def spot(c, k):
        return pl.ds(pl.multiple_of(c * (full * X) + at.x_step(k) * full + r * n, 16), n)

    got = [
        wire.send(part.at[spot(1 - at.c, k), :], core_in.at[r, o], at.core_peer())
        for o, k in enumerate(order)
    ]
    yield

    def mine(o):
        got[o].wait_recv()
        return part[spot(at.c, order[o]), :] + core_in[r, o]

    yield from ring_sum(at, wire, r, mine, half, sx, xa, x1, sz)
    swap = wire.send(sz.at[r], zin.at[r], at.h_peer())
    yield
    swap.wait_recv()
    home = spot(at.c, 0)
    total = sz[r] + zin[r]
    if keep is not None:
        keep[r] = total
    rounded = total.astype(BF)
    out[home, :] = rounded
    boards = [out]
    if stat is not None:
        kept, col = stat
        dots = jnp.sum(rounded.astype(F32) * kept[r], axis=1, keepdims=True)
        col[home, :] = jnp.broadcast_to(dots, (n, col.shape[1]))
        boards.append(col)

    def share(k, peer):
        rows_of = spot(at.c, k)
        return [wire.send(o.at[rows_of, :], o.at[rows_of, :], peer) for o in boards]

    spread = [(k, share(0, at.x_peer(k))) for k in (1, -1, 2)]
    ends = share(0, at.core_peer())
    yield
    for k, copies in spread:
        wait_all(copies)
        ends += share(-k, at.core_peer())
        if k != 1:
            yield
    wait_all(ends)


Q = 1
STREAM_COPIES = 4 + 2 + 4 + 1 + 3 + 4


def stream_scratch(rows, width):
    n = rows // (C * X * 2)
    f = lambda *s: pltpu.VMEM((*s, n, width), F32)
    return (f(2, 4), f(2, 3), f(2), f(2, 2), f(2), f(2))


def sum_exp(at, wire, value, partial, out, zbuf, ybuf):
    copies = [wire.send(value, zbuf.at[k - 1], at.z_pair(k)) for k in (1, 2, 3)]
    yield
    wait_all(copies)
    partial[...] = value[...] + zbuf[0] + zbuf[1] + zbuf[2]
    copies = [wire.send(partial, ybuf.at[i], at.y_peer(k)) for i, k in enumerate((1, -1, 2))]
    yield
    wait_all(copies)
    out[...] = partial[...] + ybuf[0] + ybuf[1] + ybuf[2]


def scatter_exp(at, wire, fill, part, out, sbuf, ya, y1, y2, sz, zin):
    rows, width = out.shape
    half = width // 2
    lo, hi = pl.ds(0, half), pl.ds(half, half)
    order = (3, 2, 1, 0)

    def spot(dy, j):
        e = at.y_step(dy) * Z + at.z_swap(order[j])
        return pl.ds(pl.multiple_of(e * rows, 16), rows)

    first, early, late = [[], [], [], []], [], []
    for lanes, side, peer in ((lo, 0, at.y_peer(1)), (hi, half, at.y_peer(-1))):
        fill(2, lanes)
        for j in range(4):
            sbuf[j, 0, :, side : side + half] = part[spot(2, j), lanes].astype(BF)
            first[j].append(wire.send(sbuf.at[j, 0, :, lanes], ya.at[j, :, lanes], peer))
        yield
    for lanes in (lo, hi):
        fill(1, lanes)
        fill(-1, lanes)
    for j in range(4):
        sbuf[j, 1, :, half:] = part[spot(1, j), hi].astype(BF)
        sbuf[j, 2, :, :half] = part[spot(-1, j), lo].astype(BF)
        early.append(
            (
                wire.send(sbuf.at[j, 1, :, hi], y1.at[j, :, hi], at.y_peer(1)),
                wire.send(sbuf.at[j, 2, :, lo], y2.at[j, :, lo], at.y_peer(-1)),
            )
        )
        first[j][0].wait_recv()
        sbuf[j, 1, :, :half] = (part[spot(1, j), lo] + ya[j, :, :half].astype(F32)).astype(BF)
        right = wire.send(sbuf.at[j, 1, :, lo], y1.at[j, :, lo], at.y_peer(1))
        first[j][1].wait_recv()
        sbuf[j, 2, :, half:] = (part[spot(-1, j), hi] + ya[j, :, half:].astype(F32)).astype(BF)
        left = wire.send(sbuf.at[j, 2, :, hi], y2.at[j, :, hi], at.y_peer(-1))
        late.append((right, left))
        yield
    for lanes in (lo, hi):
        fill(0, lanes)
    tail = []
    for j in range(4):
        yield
        wait_all(early[j] + late[j])
        total = part[spot(0, j), :] + y1[j].astype(F32) + y2[j].astype(F32)
        if order[j] == 0:
            out[...] = total
        else:
            sz[j] = total.astype(BF)
            tail.append(wire.send(sz.at[j], zin.at[j], at.z_pair(order[j])))
    yield
    wait_all(tail)
    out[...] = out[...] + zin[0].astype(F32) + zin[1].astype(F32) + zin[2].astype(F32)


def scatter_tok(at, wire, part, out, core_in, sx, xa, x1, sz, zin):
    rows = out.shape[0]
    order = (2, 1, -1, 0)

    def spot(h, k, c):
        t = h * 8 + at.x_step(k) * 2 + c
        return pl.ds(pl.multiple_of(t * rows, 16), rows)

    got = [
        [
            wire.send(part.at[spot(h, k, 1 - at.c), :], core_in.at[o, h], at.core_peer())
            for h in range(H)
        ]
        for o, k in enumerate(order)
    ]
    yield
    for copies in got:
        wait_all(copies)

    def mine(o, h):
        return part[spot(h, order[o], at.c), :] + core_in[o, h]

    for h in range(H):
        sx[0, h] = mine(0, h).astype(BF)
    a = wire.send(sx.at[0, 0], xa.at[0], at.x_peer(1))
    b = wire.send(sx.at[0, 1], xa.at[1], at.x_peer(-1))
    sx[1, 1] = mine(1, 1).astype(BF)
    sx[2, 0] = mine(2, 0).astype(BF)
    early1 = wire.send(sx.at[1, 1], x1.at[0, 1], at.x_peer(1))
    early2 = wire.send(sx.at[2, 0], x1.at[1, 0], at.x_peer(-1))
    yield
    a.wait_recv()
    sx[1, 0] = (mine(1, 0) + xa[0].astype(F32)).astype(BF)
    late1 = wire.send(sx.at[1, 0], x1.at[0, 0], at.x_peer(1))
    b.wait_recv()
    sx[2, 1] = (mine(2, 1) + xa[1].astype(F32)).astype(BF)
    late2 = wire.send(sx.at[2, 1], x1.at[1, 1], at.x_peer(-1))
    yield
    wait_all((early1, early2, late1, late2))

    def total(h):
        own = part[spot(h, 0, at.c), :] + core_in[3, h]
        return own + x1[0, h].astype(F32) + x1[1, h].astype(F32)

    sz[...] = total(1 - at.h).astype(BF)
    swap = wire.send(sz, zin, at.h_peer())
    out[...] = total(at.h)
    yield
    swap.wait_recv()
    out[...] = out[...] + zin[...].astype(F32)


def gelu_parts(pre_act):
    inner = GELU_C * (pre_act + 0.044715 * pre_act**3)
    tangent = jnp.tanh(inner)
    value = 0.5 * pre_act * (1.0 + tangent)
    slope = 0.5 * (1.0 + tangent) + 0.5 * pre_act * (1.0 - tangent * tangent) * GELU_C * (
        1.0 + 3.0 * 0.044715 * pre_act * pre_act
    )
    return (value, slope)


def nn(a, b):
    return lax.dot_general(a, b, (((1,), (0,)), ((), ())), preferred_element_type=F32)


def nt(a, b):
    return lax.dot_general(a, b, (((1,), (1,)), ((), ())), preferred_element_type=F32)


def tiles(count, size, body):
    def go(i, carry):
        body(pl.ds(pl.multiple_of(i * size, size), size))
        return carry

    lax.fori_loop(0, count, go, 0)


def advance(*gens):
    for g in gens:
        next(g, None)


ORDER = (
    "TZ", "T", "tg", "G", "GZ", "turn", "T", "T", "G", "T", "T", "T", "T", "T", "G", "G",
    "T", "c1", "G", "G", "c2", "S1", "G", "S1", "m2", "G", "S1", "G", "c3", "S2", "S1", "S2",
    "S2", "S1", "S1", "S2", "S1", "S1", "c4", "c5", "C1", "S2", "C1", "S2", "C1", "S2", "S2", "c6",
    "c7", "C2", "put", "C1", "C2", "C2", "C1", "C1", "C2", "C1", "C1", "c8", "R", "C2", "R", "C2",
    "R", "C2", "C2", "c8t", "c9a", "E", "c9b", "E", "c11", "F", "E", "E", "F", "E", "E", "F",
    "E", "E", "F", "E", "E", "F", "E", "E",
)


def kernel(
    x_in,
    g_in,
    proj_hbm,
    w_in_hbm,
    w_out_hbm,
    slot_norm,
    token_norm,
    grad_tokens,
    grad_proj,
    slot_in_out,
    slot_grad_out,
    hidden_out,
    pre_grad_out,
    *rest,
):
    rest = list(rest)

    def take(n=1):
        got = rest[:n]
        del rest[:n]
        return got if n > 1 else got[0]

    x_ref, g_ref, tok, grad, both, proj_t, w_in, w_out = take(8)
    dispatch, combine, mixed, comb_half = take(4)
    parts = take(4)
    slot_in, slot_grad, hidden, pre_grad = take(4)
    slope, slot_out, slot_in_grad, kept, col = take(5)
    cross, weighted, base, logit_half, term, proj_part = take(6)
    streams = [take(6) for _ in range(4 * Q)]
    row, row_sum, row_stat, token_row, zbuf, ybuf = take(6)
    e_bufs = take(6)
    f_bufs = take(6)
    local_sem, send_sem, recv_sem = take(3)
    slots = slot_norm.shape[0]
    tokens = token_norm.shape[0]
    width = tok.shape[0]
    tok_total = jnp.float32(tokens * X * C * H)
    all_slots = jnp.float32(slots * Y * Z)
    proj = both.at[:, pl.ds(0, slots)]
    disp_half = mixed.at[pl.ds(slots, slots), :]
    inner_half = mixed.at[pl.ds(0, slots), :]

    loads = [
        pltpu.make_async_copy(proj_hbm, proj, local_sem.at[0]),
        pltpu.make_async_copy(w_in_hbm, w_in, local_sem.at[1]),
        pltpu.make_async_copy(w_out_hbm, w_out, local_sem.at[2]),
    ]
    for load in loads:
        load.start()
    at = Places()
    x_ref[...] = x_in[...].astype(BF)
    greet(at.everyone())
    wire = Wire(send_sem, recv_sem)

    def halves(i, out, **more):
        gens = []
        for q in range(Q):
            cols = pl.ds(q * (width // Q), width // Q)
            args = (parts[i].at[:, cols], out.at[:, cols], *streams[i * Q + q])
            opts = {}
            if "keep" in more:
                opts["keep"] = kept.at[q]
            if "stat" in more:
                opts["stat"] = (kept.at[q], col.at[q])
            gens += [reduced(at, wire, r, *args, **opts) for r in range(2)]
        return gens

    def fill(k, cols):
        rows = pl.ds(pl.multiple_of(at.y_step(k) * (width // Y), 16), width // Y)
        new = nn(both[rows, :], mixed[:, cols])
        term[rows, cols] = new - row_stat[:, cols] * cross[rows, cols]

    tok_z, grad_z = [], []
    gens = {
        "TZ": [z_sends(at, wire, x_ref, tok, tok_z)],
        "GZ": [z_sends(at, wire, g_ref, grad, grad_z)],
        "T": [gather(at, wire, x_ref, tok, tok_z)],
        "G": [gather(at, wire, g_ref, grad, grad_z)],
        "S1": halves(0, slot_in, keep=True),
        "S2": halves(1, slot_grad),
        "C1": halves(2, slot_out),
        "C2": halves(3, slot_in_grad, stat=True),
        "R": [sum_exp(at, wire, row, row_sum, row_stat, zbuf, ybuf)],
        "E": [scatter_exp(at, wire, fill, term, grad_tokens, *e_bufs)],
        "F": [scatter_tok(at, wire, proj_part, grad_proj, *f_bufs)],
    }

    def c1():
        token_row[...] = token_norm[...].reshape(1, tokens)
        slot_shift = jnp.broadcast_to(slot_norm[...].reshape(1, slots), (128, slots)).T[:, :1]

        def go(cols):
            logits = nn(proj_t[...], tok[:, cols])
            d = jnp.exp(logits - slot_shift) / tok_total
            c = jnp.exp(logits - token_row[:, cols]) / all_slots
            dispatch[:, cols] = d
            combine[:, cols] = c
            mixed[pl.ds(slots, slots), cols] = d.astype(BF)
            comb_half[:, cols] = c.astype(BF)

        tiles(3, 256, go)

    def c2():
        def go(rows):
            parts[0][:, rows] = nt(disp_half[...], tok[rows, :])

        tiles(5, 256, go)

    def c3():
        def go(rows):
            parts[1][:, rows] = nt(comb_half[...], grad[rows, :])

        tiles(5, 256, go)

    def m2():
        def go(rows):
            cross[rows, :] = nn(both[rows, pl.ds(0, slots)], comb_half[...])

        tiles(5, 256, go)

    def c4():
        loads[1].wait()
        value, s = gelu_parts(nt(slot_in[...], w_in[...]))
        hidden[...] = value.astype(BF)
        slope[...] = s

    def c5():
        loads[2].wait()

        def go(cols):
            parts[2][:, cols] = nn(hidden[...], w_out[:, cols])

        tiles(5, 256, go)

    def c6():
        pre_grad[...] = (nt(slot_grad[...], w_out[...]) * slope[...]).astype(BF)

    def c7():
        def go(cols):
            parts[3][:, cols] = nn(pre_grad[...], w_in[:, cols])

        tiles(5, 256, go)

    def c8():
        def go(cols):
            w = combine[:, cols] * nn(slot_out[...], grad[:, cols])
            weighted[:, cols] = w
            row[:, cols] = jnp.sum(w, axis=0, keepdims=True)

        tiles(3, 256, go)

    def c8t():
        def go(cols):
            both[cols, pl.ds(slots, slots)] = slot_in_grad[:, cols].T

        tiles(5, 256, go)

    def c9(i):
        cols = pl.ds(i * (tokens // 2), tokens // 2)
        disp_grad = nn(slot_in_grad[...], tok[:, cols])
        b = weighted[:, cols] + dispatch[:, cols] * (disp_grad - jnp.sum(col[...], axis=0)[:, :1])
        base[:, cols] = b
        mixed[pl.ds(0, slots), cols] = b.astype(BF)

    def c11():
        def make(cols):
            logit_half[:, cols] = (base[:, cols] - combine[:, cols] * row_stat[:, cols]).astype(BF)

        tiles(3, 256, make)

        def go(rows):
            proj_part[rows, :] = nt(tok[rows, :], logit_half[...])

        tiles(5, 256, go)

    def turn():
        loads[0].wait()

        def go(rows):
            proj_t[:, rows] = both[rows, pl.ds(0, slots)].T

        tiles(5, 256, go)

    def tg():
        g_ref[...] = g_in[...].astype(BF)

    kept_for_weights = (
        (slot_in, slot_in_out),
        (slot_grad, slot_grad_out),
        (hidden, hidden_out),
        (pre_grad, pre_grad_out),
    )
    stores = [
        pltpu.make_async_copy(held, out, local_sem.at[3 + i])
        for i, (held, out) in enumerate(kept_for_weights)
    ]

    def put():
        for store in stores:
            store.start()

    work = dict(put=put, turn=turn, tg=tg, c1=c1, c2=c2, c3=c3, c4=c4, c5=c5, c6=c6, c7=c7, c8=c8, c8t=c8t, c9a=lambda: c9(0), c9b=lambda: c9(1), c11=c11, m2=m2)
    for name in ORDER:
        if name in work:
            work[name]()
        else:
            advance(*gens[name])
    assert all(next(g, None) is None and g.gi_frame is None for gs in gens.values() for g in gs)
    for store in stores:
        store.wait()
    wire.drain()


def fused(x, g, slot_proj, w_in, w_out, slot_norm, token_norm):
    rows, n = x.shape
    width, slots = slot_proj.shape
    ff = w_in.shape[0]
    prows = width // 16
    b = lambda *s: pltpu.VMEM(s, BF)
    f = lambda *s: pltpu.VMEM(s, F32)
    part = f(slots, width)
    scratch = (
        *(b(rows, n), b(rows, n)),
        *(b(width, n), b(width, n), b(width, 2 * slots), b(slots, width), b(ff, width), b(ff, width)),
        *(f(slots, n), f(slots, n), b(2 * slots, n), b(slots, n)),
        *(part, part, part, part),
        *(b(slots, width), b(slots, width), b(slots, ff), b(slots, ff)),
        *(f(slots, ff), b(slots, width), b(slots, width), f(Q, 2, slots // 16, width // Q), f(Q, slots, 128)),
        *(f(width, n), f(slots, n), f(slots, n), b(slots, n), f(width, n), f(width, slots)),
        *(stream_scratch(slots, width // Q) * (4 * Q)),
        *(f(1, n), f(1, n), f(1, n), f(1, n), f(3, 1, n), f(3, 1, n)),
        *(b(4, 3, rows, n), b(4, rows, n), b(4, rows, n), b(4, rows, n), b(3, rows, n), b(3, rows, n)),
        f(4, H, prows, slots),
        *(b(3, H, prows, slots), b(H, prows, slots), b(2, H, prows, slots)),
        *(b(prows, slots), b(prows, slots)),
    )
    copies = 38 + 8 * Q * STREAM_COPIES + 14 * Q + 6 + 27 + 15
    any_space = pl.BlockSpec(memory_space=pl.ANY)
    outs = (
        ((rows, n), F32),
        ((prows, slots), F32),
        ((slots, width), BF),
        ((slots, width), BF),
        ((slots, ff), BF),
        ((slots, ff), BF),
    )
    return pl.pallas_call(
        kernel,
        out_shape=tuple(jax.ShapeDtypeStruct(s, d) for s, d in outs),
        in_specs=[VMEM, VMEM, any_space, any_space, any_space, VMEM, VMEM],
        out_specs=(VMEM, VMEM, any_space, any_space, any_space, any_space),
        scratch_shapes=[
            *scratch,
            pltpu.SemaphoreType.DMA((7,)),
            pltpu.SemaphoreType.DMA((copies,)),
            pltpu.SemaphoreType.DMA((copies,)),
        ],
        compiler_params=pltpu.CompilerParams(
            collective_id=0, has_side_effects=True, vmem_limit_bytes=60000 * 1024
        ),
    )(x, g, slot_proj, w_in, w_out, slot_norm, token_norm)


dot = functools.partial(jnp.einsum, preferred_element_type=jnp.float32)


def local(tokens, out_grad, slot_proj, weight_in, weight_out, slot_norm, token_norm):
    grad_tokens, grad_slot_proj, slot_in, slot_grad, hidden, pre_grad = fused(
        tokens.T,
        out_grad.T,
        slot_proj,
        weight_in[0].T,
        weight_out[0],
        slot_norm,
        token_norm,
    )
    grad_weight_out = dot("sf,sd->fd", hidden, slot_grad)
    grad_weight_in = dot("sd,sf->df", slot_in, pre_grad)
    return (grad_tokens.T, grad_slot_proj, grad_weight_in[None], grad_weight_out[None])


def solution(mesh):
    return jax.shard_map(
        local,
        mesh=mesh,
        in_specs=(
            P("tok", "exp"),
            P("tok", "exp"),
            P(None, "exp"),
            P("exp", None, "tok"),
            P("exp", "tok", None),
            P("exp"),
            P("tok"),
        ),
        out_specs=(P("tok", "exp"), P("tok", "exp"), P("exp", None, "tok"), P("exp", "tok", None)),
        check_vma=False,
    )
```
